512 devices in a mesh: dp: 64 (over x, z), inner: 8 (over y, core).
Axes of the slice: x: 4, y: 4, z: 16, core: 2. Of those that a mesh axis runs over, the one named last changes fastest.
Arguments:
- tokens: bfloat16 [4096, 2880], P(('dp', 'inner')), may hold values from -6 to 6
- segments: int32 [4096], P(('dp', 'inner')), may hold values from 0 to 63, never falling along the last dimension, each value on 1 to 256 neighbouring positions
- attn_gain: float32 [2880], replicated, may hold values from 0.5 to 1.5
- w_query: bfloat16 [2880, 4096], P('dp', 'inner'), may hold values from -0.109375 to 0.109375
- w_keyval: bfloat16 [2880, 1024], P('dp', 'inner'), may hold values from -0.109375 to 0.109375
- sink_logits: float32 [64], P('inner'), may hold values from -1 to 3
- w_out: bfloat16 [4096, 2880], P('inner', 'dp'), may hold values from -0.09375 to 0.09375
- moe_gain: float32 [2880], replicated, may hold values from 0.5 to 1.5
- w_router: bfloat16 [2880, 32], replicated, may hold values from -0.109375 to 0.109375
- routes: int32 [4096, 4], P(('dp', 'inner')), may hold values from 0 to 31, all different within a row; in each aligned block of 8 rows (0 to 7, 8 to 15, ...) at most 2 rows name the same one
- w_gate_up: bfloat16 [92160, 5760], P('dp', 'inner'), may hold values from -0.109375 to 0.109375
- b_gate_up: float32 [32, 5760], P(None, 'inner'), may hold values from -3 to 3
- w_down: bfloat16 [2880, 92160], P('inner', 'dp'), may hold values from -0.109375 to 0.109375
- b_down: float32 [32, 2880], replicated, may hold values from -3 to 3
Outputs:
- layer_out: bfloat16 [4096, 2880], P(('dp', 'inner'))
The draws below stay inside these ranges and needn't reach their ends.
Inputs may be any that keep to these rules, and one draw needn't show every extreme that they name: `routes`: in each aligned block of 8 rows (the rows of one device) no expert is named by more than 2 rows, a bound that some block reaches; the 4 experts of a row differ. `segments`: never falling along the tokens; each segment holds 1 to 256 tokens, one exactly 256.
All inputs are finite; a program needn't handle non-finite values.
Results may differ from the reference program's by a relative error of at most 0.018.
Values may be sent and summed in bfloat16 or wider, within the bound.
A program may use at most 64 MiB of HBM per device.

```python
import math
import jax
import jax.numpy as jnp
import numpy as np
from jax import lax

D = 2880
HEADS = 64
KV_HEADS = 8
HEAD_DIM = 64
FF = 2880
TOP = 4
WINDOW = 128
TOK_DEV = 8
EXPERTS = 32
TOKENS = 4096
CAP = 2
SEG_MOST = 256
N_DP = 64
N_INNER = 8


def shard_levels(own_key, extent, cuts, low, largest):
    def one(dim, parts):
        heights = jax.random.uniform(jax.random.fold_in(jax.random.fold_in(own_key, 6), dim), (parts,), jnp.float32, low / len(cuts), largest / len(cuts))
        return jnp.repeat(jnp.exp(heights), extent[dim] // parts).reshape((-1,) + (1,) * (len(extent) - dim - 1))

    factor_of = one(*cuts[0])
    for cut in cuts[1:]:
        factor_of = factor_of * one(*cut)
    return factor_of


def length_profile(amount, total, reach, slope):
    loads = [(1 << 20) // math.isqrt(rank ** slope) + 1 for rank in range(2, amount + 1)]
    spare, given = total - reach - (amount - 1), [1] * (amount - 1)
    while spare > 0:
        free = [i for i in range(amount - 1) if given[i] < reach]
        whole, left = sum([loads[i] for i in free]), spare
        for i in free:
            extra = min(reach - given[i], max(1, left * loads[i] // whole), spare)
            given[i] = given[i] + extra
            spare = spare - extra
    return np.array([reach] + given)


def ragged(key, amount, total, bound, skew):
    if amount == 2:
        one = jax.random.randint(key, (), max(1, total - bound), min(bound, total - 1) + 1)
        return jnp.stack([one, total - one])
    sizes = jnp.asarray(length_profile(amount, total, bound, skew), jnp.int32)
    couples = (amount - 1) // 2
    giver, sink = sizes[1:1 + 2 * couples:2], sizes[2:2 + 2 * couples:2]
    room = jnp.minimum(giver - 1, bound - sink)
    shifted = jax.random.randint(jax.random.fold_in(key, 1), (couples,), 0, 1 << 20) % (room + 1)
    sizes = sizes.at[1:1 + 2 * couples:2].set(giver - shifted).at[2:2 + 2 * couples:2].set(sink + shifted)
    return sizes[jax.random.permutation(jax.random.fold_in(key, 2), amount)]


def shared_out(own_key, own, number, rows, amount, top, bound, lean):
    order = jax.random.permutation(own_key, amount)
    crowded, usual = portions_of(amount, rows * top, bound, lean, True), portions_of(amount, rows * top, bound, lean, False)
    places = jnp.arange(amount)

    def named(tallies, rotation):
        used = int((tallies > 0).sum())
        fixed = max(1, used // 4)
        shifted = fixed + (places - fixed + rotation * (used - fixed)) % max(1, amount - fixed)
        return jnp.zeros((amount,), jnp.int32).at[order[jnp.where(places < fixed, places, shifted)]].set(jnp.asarray(tallies, jnp.int32))

    tallies = jnp.where(number % 4 == 0, named(crowded, number // 4), named(usual, number - number // 4 - 1))
    mixed = jax.random.permutation(jax.random.fold_in(own, 3), amount)
    source_of, taker = mixed[0:amount // 2 * 2:2], mixed[1:amount // 2 * 2:2]
    margin = jnp.minimum(tallies[source_of] - 1, bound - tallies[taker]) // 2
    margin = jnp.where((source_of == order[0]) | (taker == order[0]) | (tallies[taker] == 0), 0, jnp.maximum(margin, 0))
    shifted = jax.random.randint(jax.random.fold_in(own, 4), (amount // 2,), 0, 1 << 20) % (margin + 1)
    tallies = tallies.at[source_of].add(-shifted).at[taker].add(shifted)
    members = jnp.searchsorted(jnp.cumsum(tallies), jnp.arange(rows * top), side="right").astype(jnp.int32)
    table = members.reshape(top, rows).T
    table = table[jax.random.permutation(jax.random.fold_in(own, 1), rows)]
    rotation = jax.random.randint(jax.random.fold_in(own, 2), (rows, 1), 0, top)
    return jnp.take_along_axis(table, (jnp.arange(top)[None, :] + rotation) % top, axis=1)


def portions_of(number_of, total, bound, lean, full):
    weights = [(1 << 20) // math.isqrt(rank ** lean) + 1 for rank in range(1, number_of + 1)]
    largest = bound if full else min(bound, max(-(-total // number_of), total * weights[0] // sum(weights)))
    least = 1 if total - largest >= number_of - 1 else 0
    holding, spare = [largest] + [least] * (number_of - 1), total - largest - least * (number_of - 1)
    while spare > 0:
        candidates = [i for i in range(1, number_of) if holding[i] < largest] or [i for i in range(1, number_of) if holding[i] < bound]
        mass, remaining = sum([weights[i] for i in candidates]), spare
        for i in candidates:
            extra = min(bound - holding[i], max(1, remaining * weights[i] // mass), spare)
            holding[i] = holding[i] + extra
            spare = spare - extra
    return np.array(holding)


def centred(stream_key, extent, width, reach, cuts=(), kind=jnp.bfloat16):
    gain = shard_levels(stream_key, extent, cuts, -0.22, 0.18) if cuts else 1.0
    values = jax.random.normal(stream_key, extent, jnp.float32) * width * gain
    return jnp.minimum(jnp.maximum(values, -reach), reach).astype(kind)


def setup_inputs(seed: int = 0) -> dict:
    keys = jax.random.split(jax.random.key(seed), 15)
    tokens = centred(keys[0], (TOKENS, D), 1.0, 6.0, ((0, 512),))
    segments = jnp.searchsorted(jnp.cumsum(ragged(keys[1], TOKENS // 64, TOKENS, SEG_MOST, 2)), jnp.arange(TOKENS), side="right").astype(jnp.int32)
    attn_gain = jnp.clip(1.0 + 0.1 * jax.random.normal(keys[2], (D,), jnp.float32), 0.5, 1.5)
    w_query = centred(keys[3], (D, HEADS * HEAD_DIM), D ** -0.5, 0.109375, ((0, 64), (1, 8)))
    w_keyval = centred(keys[4], (D, 2 * KV_HEADS * HEAD_DIM), D ** -0.5, 0.109375, ((0, 64), (1, 8)))
    sink_logits = jnp.clip(-1.0 + 4.0 * jax.random.uniform(keys[5], (HEADS,), jnp.float32) ** shard_levels(keys[5], (HEADS,), ((0, 8),), -0.2, 0.2), -1.0, 3.0)
    w_out = centred(keys[6], (HEADS * HEAD_DIM, D), (HEADS * HEAD_DIM) ** -0.5, 0.09375, ((0, 8), (1, 64)))
    moe_gain = jnp.clip(1.0 + 0.1 * jax.random.normal(keys[7], (D,), jnp.float32), 0.5, 1.5)
    w_router = centred(keys[8], (D, EXPERTS), D ** -0.5, 0.109375)
    routes_keys = jax.random.split(jax.random.fold_in(keys[9], 1), TOKENS // TOK_DEV)
    routes_turns = jax.random.permutation(jax.random.fold_in(keys[9], 3), TOKENS // TOK_DEV)
    routes = jax.vmap(lambda own, number: shared_out(jax.random.fold_in(keys[9], 2), own, number, TOK_DEV, EXPERTS, TOP, CAP, 2))(routes_keys, routes_turns).reshape((TOKENS, TOP))
    w_gate_up = centred(keys[10], (EXPERTS * D, 2 * FF), D ** -0.5, 0.109375, ((0, 64), (1, 8)))
    b_gate_up = centred(keys[11], (EXPERTS, 2 * FF), 0.5, 3.0, ((1, 8),), jnp.float32)
    w_down = centred(keys[12], (FF, EXPERTS * D), FF ** -0.5, 0.109375, ((0, 8), (1, 64)))
    b_down = centred(keys[13], (EXPERTS, D), 0.5, 3.0, (), jnp.float32)
    return dict(tokens=tokens, segments=segments, attn_gain=attn_gain, w_query=w_query, w_keyval=w_keyval, sink_logits=sink_logits, w_out=w_out, moe_gain=moe_gain, w_router=w_router, routes=routes, w_gate_up=w_gate_up, b_gate_up=b_gate_up, w_down=w_down, b_down=b_down)


EPSILON = 1e-05
ROPE_BASE = 150000.0
CLAMP_LIMIT = 7.0
GLU_SLOPE = 1.702

def rms_scale(row_block, gain_vector):
    values = row_block.astype(jnp.float32)
    mean_square = lax.optimization_barrier(jnp.mean(values * values, axis=-1, keepdims=True))
    return (values * lax.rsqrt(mean_square + EPSILON) * gain_vector).astype(jnp.bfloat16)

def rotate(values, positions):
    half_dim = values.shape[-1] // 2
    frequency = ROPE_BASE ** (-2.0 * jnp.arange(half_dim, dtype=jnp.float32) / values.shape[-1])
    angles = positions.astype(jnp.float32)[:, None] * frequency[None, :]
    cosine = jnp.cos(angles)[:, None, :]
    sine_part = jnp.sin(angles)[:, None, :]
    first_half = values[..., :half_dim]
    second = values[..., half_dim:]
    return jnp.concatenate([first_half * cosine - second * sine_part, second * cosine + first_half * sine_part], axis=-1)

def attend(queries, key_block, value_block, sink_heads, query_pos, key_pos, query_seg, key_seg):
    scores = jnp.einsum('qgph,kgh->gpqk', queries.astype(jnp.float32), key_block.astype(jnp.float32)) * HEAD_DIM ** (-0.5)
    distance = query_pos[:, None] - key_pos[None, :]
    allowed = (distance >= 0) & (distance < WINDOW) & (key_pos[None, :] >= 0) & (query_seg[:, None] == key_seg[None, :])
    scores = jnp.where(allowed[None, None], scores, -jnp.inf)
    row_max = jnp.maximum(lax.optimization_barrier(jnp.max(scores, axis=-1)), sink_heads[:, :, None])
    weights = jnp.exp(scores - row_max[..., None])
    denominator = lax.optimization_barrier(jnp.sum(weights, axis=-1)) + jnp.exp(sink_heads[:, :, None] - row_max)
    probabilities = (weights / denominator[..., None]).astype(jnp.bfloat16)
    mixed_heads = jnp.einsum('gpqk,kgh->qgph', probabilities.astype(jnp.float32), value_block.astype(jnp.float32))
    return mixed_heads.astype(jnp.bfloat16)

def reference(tokens, segments, attn_gain, w_query, w_keyval, sink_logits, w_out, moe_gain, w_router, routes, w_gate_up, b_gate_up, w_down, b_down):
    per_kv = HEADS // KV_HEADS
    attn_in = rms_scale(tokens, attn_gain)
    positions = jnp.arange(TOKENS, dtype=jnp.int32)
    query_acc = jnp.dot(attn_in, w_query, preferred_element_type=jnp.float32).reshape(TOKENS, HEADS, HEAD_DIM)
    keyval = jnp.dot(attn_in, w_keyval, preferred_element_type=jnp.float32).reshape(TOKENS, KV_HEADS, 2, HEAD_DIM)
    queries = rotate(query_acc, positions).astype(jnp.bfloat16).reshape(TOKENS, KV_HEADS, per_kv, HEAD_DIM)
    key_rows = rotate(keyval[:, :, 0], positions).astype(jnp.bfloat16)
    value_rows = keyval[:, :, 1].astype(jnp.bfloat16)
    key_pad = jnp.concatenate([jnp.zeros((WINDOW, KV_HEADS, HEAD_DIM), jnp.bfloat16), key_rows], axis=0)
    value_pad = jnp.concatenate([jnp.zeros((WINDOW, KV_HEADS, HEAD_DIM), jnp.bfloat16), value_rows], axis=0)
    seg_pad = jnp.concatenate([jnp.full((WINDOW,), -1, jnp.int32), segments.astype(jnp.int32)], axis=0)
    sink_heads = sink_logits.reshape(KV_HEADS, per_kv)

    def one_block(block_index):
        first_row = (block_index * WINDOW).astype(jnp.int32)
        block_queries = lax.dynamic_slice_in_dim(queries, first_row, WINDOW, 0)
        block_keys = lax.dynamic_slice_in_dim(key_pad, first_row, 2 * WINDOW, 0)
        block_values = lax.dynamic_slice_in_dim(value_pad, first_row, 2 * WINDOW, 0)
        key_seg = lax.dynamic_slice_in_dim(seg_pad, first_row, 2 * WINDOW, 0)
        query_seg = lax.dynamic_slice_in_dim(segments.astype(jnp.int32), first_row, WINDOW, 0)
        query_pos = first_row + jnp.arange(WINDOW, dtype=jnp.int32)
        key_pos = first_row - WINDOW + jnp.arange(2 * WINDOW, dtype=jnp.int32)
        return attend(block_queries, block_keys, block_values, sink_heads, query_pos, key_pos, query_seg, key_seg)
    attended = lax.map(one_block, jnp.arange(TOKENS // WINDOW, dtype=jnp.int32))
    attended = attended.reshape(TOKENS, HEADS * HEAD_DIM)
    residual = (tokens.astype(jnp.float32) + jnp.dot(attended, w_out, preferred_element_type=jnp.float32)).astype(jnp.bfloat16)
    moe_in = rms_scale(residual, moe_gain)
    logits = jnp.dot(moe_in, w_router, preferred_element_type=jnp.float32)
    chosen = jnp.take_along_axis(logits, routes, axis=1)
    mix = jax.nn.softmax(chosen, axis=-1)
    flat_mix = mix.reshape(-1)
    flat_routes = routes.reshape(-1)
    limit = N_DP * N_INNER * CAP
    block_width = FF // N_INNER
    half_width = D // 2

    def add_expert(totals, expert):
        hit_mask = flat_routes == expert
        hit_rows = jnp.nonzero(hit_mask, size=limit, fill_value=0)[0].astype(jnp.int32)
        live = (jnp.arange(limit, dtype=jnp.int32) < jnp.sum(hit_mask.astype(jnp.int32))).astype(jnp.float32)
        token_ids = hit_rows // TOP
        row_block = moe_in[token_ids]
        gate_weight = lax.dynamic_slice_in_dim(w_gate_up, (expert * D).astype(jnp.int32), D, 0)
        first_part = jnp.dot(row_block[:, :half_width], gate_weight[:half_width], preferred_element_type=jnp.float32).astype(jnp.bfloat16)
        second_part = jnp.dot(row_block[:, half_width:], gate_weight[half_width:], preferred_element_type=jnp.float32).astype(jnp.bfloat16)
        first_part, second_part = lax.optimization_barrier((first_part, second_part))
        gate_up = first_part.astype(jnp.float32) + second_part.astype(jnp.float32) + b_gate_up[expert]
        gate_part = jnp.minimum(gate_up[:, 0::2], CLAMP_LIMIT)
        up_part = jnp.clip(gate_up[:, 1::2], -CLAMP_LIMIT, CLAMP_LIMIT)
        hidden = ((up_part + 1.0) * gate_part * jax.nn.sigmoid(GLU_SLOPE * gate_part)).astype(jnp.bfloat16)
        down_weight = lax.dynamic_slice_in_dim(w_down, (expert * D).astype(jnp.int32), D, 1)
        pieces = jnp.einsum('rnf,nfd->rnd', hidden.reshape(limit, N_INNER, block_width).astype(jnp.float32), down_weight.reshape(N_INNER, block_width, D).astype(jnp.float32))
        expert_out = lax.optimization_barrier(jnp.sum(pieces.astype(jnp.bfloat16), axis=1, dtype=jnp.float32)) + b_down[expert]
        scaled = flat_mix[hit_rows] * live
        return (totals.at[token_ids].add(scaled[:, None] * expert_out), None)
    moe_sum = lax.scan(add_expert, jnp.zeros((TOKENS, D), jnp.float32), jnp.arange(EXPERTS, dtype=jnp.int32))[0]
    return (residual.astype(jnp.float32) + moe_sum).astype(jnp.bfloat16)
```

```python
import functools
import jax
import jax.numpy as jnp
from jax import lax
from jax.experimental import pallas as pl
from jax.experimental.pallas import tpu as pltpu
from jax.sharding import PartitionSpec as P

HEAD_DIM = 64
WINDOW = 128
MESH = pl.DeviceIdType.MESH

EPSILON = 1e-05
ROPE_BASE = 150000.0
CLAMP_LIMIT = 7.0
GLU_SLOPE = 1.702

NX = 4
NZ = 16
NI = 8
NDP = NX * NZ
ROWS = 8
GROUP = ROWS * NI
KPART = 45
KPAD = 48
QUART = NZ * KPAD
HEADS_HERE = 8
QCOLS = HEADS_HERE * HEAD_DIM
KVCOLS = 2 * HEAD_DIM
D = NX * NZ * KPART


def attention_kernel(
    tok_ref,
    gain_ref,
    seg_ref,
    wqkv_ref,
    wout_ref,
    cos_ref,
    sin_ref,
    sink_ref,
    res_ref,
    norm,
    wide,
    quarter,
    rows_in,
    wq_all,
    wo_all,
    part_f,
    part_out,
    part_in,
    seg_f,
    keyval,
    attended,
    out_part,
    out_in,
    ring_send,
    ring_recv,
    row_send,
    row_recv,
    part_send,
    part_recv,
    key_send,
    key_recv,
    att_send,
    att_recv,
    out_send,
    out_recv,
):
    dp = lax.axis_index("dp")
    inner = lax.axis_index("inner")
    x = dp // NZ
    z = dp % NZ
    right = x * NZ + (z + 1) % NZ
    left = x * NZ + (z + NZ - 1) % NZ

    barrier = pltpu.get_barrier_semaphore()

    def greet(index, carry):
        other_dp = ((x + index // NI) % NX) * NZ + z
        other_in = (inner + index % NI) % NI
        pl.semaphore_signal(barrier, inc=1, device_id=(other_dp, other_in), device_id_type=MESH)
        return carry

    lax.fori_loop(1, NX * NI, greet, 0)
    for other in (
        right,
        left,
        (dp + 1) % NDP,
        (dp + NDP - 1) % NDP,
        (dp + 2) % NDP,
        (dp + NDP - 2) % NDP,
    ):
        pl.semaphore_signal(barrier, inc=1, device_id=(other, inner), device_id_type=MESH)

    wq_all[z] = wqkv_ref[...]
    wo_all[z] = wout_ref[...]
    pl.semaphore_wait(barrier, NX * NI - 1 + 6)

    def ring(buffer, lane, step, towards, to):
        owner = (z + NZ - towards * (step - 1)) % NZ
        return pltpu.make_async_remote_copy(
            src_ref=buffer.at[owner],
            dst_ref=buffer.at[owner],
            send_sem=ring_send.at[lane, step - 1],
            recv_sem=ring_recv.at[lane, step - 1],
            device_id=(to, inner),
            device_id_type=MESH,
        )

    lanes = (
        (wq_all, 0, 1, right, 8),
        (wq_all, 1, -1, left, 7),
        (wo_all, 2, 1, right, 7),
        (wo_all, 3, -1, left, 8),
    )
    for buffer, lane, towards, to, last in lanes:
        ring(buffer, lane, 1, towards, to).start()

    values = tok_ref[...].astype(jnp.float32)
    mean_square = jnp.mean(values * values, axis=-1, keepdims=True)
    norm[...] = values * lax.rsqrt(mean_square + EPSILON) * gain_ref[...]
    wide[...] = jnp.zeros_like(wide)
    for block in range(NX * NZ):
        wide[:, block * KPAD : block * KPAD + KPART] = norm[:, block * KPART : (block + 1) * KPART]
    for part in range(NX):
        wide[:, part * QUART + KPART : part * QUART + KPART + 1] = seg_ref[...]
    for part in range(NX):
        quarter[part] = wide[:, part * QUART : (part + 1) * QUART].astype(jnp.bfloat16)

    def row_copy(index):
        other_x = (x + index // NI) % NX
        other_in = (inner + index % NI) % NI
        return pltpu.make_async_remote_copy(
            src_ref=quarter.at[other_x],
            dst_ref=rows_in.at[x * NI + inner],
            send_sem=row_send.at[index],
            recv_sem=row_recv.at[index],
            device_id=(other_x * NZ + z, other_in),
            device_id_type=MESH,
        )

    def start_row(index, carry):
        row_copy(index).start()
        return carry

    lax.fori_loop(1, NX * NI, start_row, 0)
    rows_in[x * NI + inner] = quarter[x]

    for step in range(1, 9):
        for buffer, lane, towards, to, last in lanes:
            if step <= last:
                ring(buffer, lane, step, towards, to).wait_recv()
            if step + 1 <= last:
                ring(buffer, lane, step + 1, towards, to).start()

    def wait_row(index, carry):
        row_copy(index).wait_recv()
        return carry

    lax.fori_loop(1, NX * NI, wait_row, 0)

    all_rows = rows_in[...].astype(jnp.float32).reshape(NX * GROUP, QUART)
    seg_f[...] = all_rows[:, :128].reshape(NX, GROUP, 128)
    product = jnp.dot(
        all_rows.astype(jnp.bfloat16),
        wq_all[...].reshape(QUART, QCOLS + KVCOLS),
        preferred_element_type=jnp.float32,
    ).reshape(NX, GROUP, QCOLS + KVCOLS)
    part_f[...] = product
    part_out[...] = product.astype(jnp.bfloat16)

    def part_copy(ahead):
        other = (x + ahead) % NX
        return pltpu.make_async_remote_copy(
            src_ref=part_out.at[other],
            dst_ref=part_in.at[ahead - 1],
            send_sem=part_send.at[ahead - 1],
            recv_sem=part_recv.at[ahead - 1],
            device_id=(other * NZ + z, inner),
            device_id_type=MESH,
        )

    for ahead in range(1, NX):
        part_copy(ahead).start()
    total = part_f[x]
    for ahead in range(1, NX):
        part_copy(ahead).wait_recv()
        total = total + part_in[ahead - 1].astype(jnp.float32)

    width = QCOLS + KVCOLS
    cosine = jnp.concatenate([cos_ref[:, :128]] * 4 + [cos_ref[:, 128:]], axis=1)
    sine = jnp.concatenate([sin_ref[:, :128]] * 4 + [sin_ref[:, 128:]], axis=1)
    column = lax.broadcasted_iota(jnp.int32, (GROUP, width), 1)
    swapped = jnp.where(
        column % HEAD_DIM < HEAD_DIM // 2,
        pltpu.roll(total, width - HEAD_DIM // 2, 1),
        pltpu.roll(total, HEAD_DIM // 2, 1),
    )
    turned = (total * cosine + swapped * sine).astype(jnp.bfloat16)
    own_seg = seg_f[x][:, KPART : KPART + 1]
    keyval[2, :, :KVCOLS] = turned[:, QCOLS:]
    keyval[2, :, KVCOLS:] = jnp.broadcast_to(own_seg, (GROUP, 128)).astype(jnp.bfloat16)

    def key_copy(ahead):
        return pltpu.make_async_remote_copy(
            src_ref=keyval.at[2],
            dst_ref=keyval.at[2 - ahead],
            send_sem=key_send.at[ahead - 1],
            recv_sem=key_recv.at[ahead - 1],
            device_id=((dp + ahead) % NDP, inner),
            device_id_type=MESH,
        )

    for ahead in (1, 2):
        key_copy(ahead).start()
    for ahead in (1, 2):
        key_copy(ahead).wait_recv()

    count = 3 * GROUP
    window = keyval[...].reshape(count, KVCOLS + 128)
    key_block = window[:, :HEAD_DIM]
    value_block = window[:, HEAD_DIM:KVCOLS]
    nt = (((1,), (1,)), ((), ()))
    key_seg = lax.dot_general(
        jnp.ones((GROUP, 128), jnp.bfloat16),
        window[:, KVCOLS:],
        nt,
        preferred_element_type=jnp.float32,
    )
    row = lax.broadcasted_iota(jnp.int32, (GROUP, count), 0)
    key = lax.broadcasted_iota(jnp.int32, (GROUP, count), 1)
    distance = row + 2 * GROUP - key
    allowed = (
        (distance >= 0)
        & (distance < WINDOW)
        & (key + (dp - 2) * GROUP >= 0)
        & (key_seg == own_seg * 128.0)
    )
    for head in range(HEADS_HERE):
        scores = lax.dot_general(
            turned[:, head * HEAD_DIM : (head + 1) * HEAD_DIM],
            key_block,
            nt,
            preferred_element_type=jnp.float32,
        ) * HEAD_DIM ** (-0.5)
        scores = jnp.where(allowed, scores, -1e30)
        sink = sink_ref[head]
        row_max = jnp.maximum(jnp.max(scores, axis=-1, keepdims=True), sink)
        weights = jnp.exp(scores - row_max)
        denominator = jnp.sum(weights, axis=-1, keepdims=True) + jnp.exp(sink - row_max)
        probabilities = (weights / denominator).astype(jnp.bfloat16)
        mixed = jnp.dot(probabilities, value_block, preferred_element_type=jnp.float32)
        attended[x, :, head * HEAD_DIM : (head + 1) * HEAD_DIM] = mixed.astype(jnp.bfloat16)

    def att_copy(ahead):
        return pltpu.make_async_remote_copy(
            src_ref=attended.at[x],
            dst_ref=attended.at[x],
            send_sem=att_send.at[ahead - 1],
            recv_sem=att_recv.at[ahead - 1],
            device_id=(((x + ahead) % NX) * NZ + z, inner),
            device_id_type=MESH,
        )

    for ahead in range(1, NX):
        att_copy(ahead).start()
    for ahead in range(1, NX):
        att_copy(ahead).wait_recv()
    projected = lax.dot_general(
        attended[...].reshape(NX * GROUP, QCOLS),
        wo_all[...].reshape(QUART, QCOLS),
        nt,
        preferred_element_type=jnp.float32,
    )
    out_part[...] = projected.reshape(NX * NI, ROWS, QUART).astype(jnp.bfloat16)

    def out_copy(index):
        other_x = (x + index // NI) % NX
        other_in = (inner + index % NI) % NI
        return pltpu.make_async_remote_copy(
            src_ref=out_part.at[other_x * NI + other_in],
            dst_ref=out_in.at[x * NI + inner],
            send_sem=out_send.at[index],
            recv_sem=out_recv.at[index],
            device_id=(other_x * NZ + z, other_in),
            device_id_type=MESH,
        )

    def start_out(index, carry):
        out_copy(index).start()
        return carry

    def wait_out(index, carry):
        out_copy(index).wait_recv()
        return carry

    lax.fori_loop(1, NX * NI, start_out, 0)
    out_in[x * NI + inner] = out_part[x * NI + inner]
    lax.fori_loop(1, NX * NI, wait_out, 0)
    summed = jnp.sum(
        out_in[...].astype(jnp.float32).reshape(NX, NI, ROWS, QUART), axis=1
    )
    for part in range(NX):
        wide[:, part * QUART : (part + 1) * QUART] = summed[part]
    for block in range(NX * NZ):
        norm[:, block * KPART : (block + 1) * KPART] = wide[:, block * KPAD : block * KPAD + KPART]
    res_ref[...] = (tok_ref[...].astype(jnp.float32) + norm[...]).astype(jnp.bfloat16)

    for buffer, lane, towards, to, last in lanes:
        for step in range(1, last + 1):
            ring(buffer, lane, step, towards, to).wait_send()

    def wait_sends(index, carry):
        row_copy(index).wait_send()
        out_copy(index).wait_send()
        return carry

    lax.fori_loop(1, NX * NI, wait_sends, 0)
    for ahead in range(1, NX):
        part_copy(ahead).wait_send()
        att_copy(ahead).wait_send()
    for ahead in (1, 2):
        key_copy(ahead).wait_send()


def rope_tables(dp_index):
    half = HEAD_DIM // 2
    frequency = ROPE_BASE ** (-2.0 * jnp.arange(half, dtype=jnp.float32) / HEAD_DIM)
    positions = dp_index * GROUP + jnp.arange(GROUP, dtype=jnp.int32)
    angles = positions.astype(jnp.float32)[:, None] * frequency[None, :]
    cosine = jnp.cos(angles)
    sine = jnp.sin(angles)
    ones = jnp.ones((GROUP, HEAD_DIM), jnp.float32)
    head_cos = jnp.concatenate([cosine, cosine], axis=1)
    head_sin = jnp.concatenate([-sine, sine], axis=1)
    return (
        jnp.concatenate([head_cos, head_cos, head_cos, ones], axis=1),
        jnp.concatenate([head_sin, head_sin, head_sin, 0.0 * ones], axis=1),
    )


def attention_layer(tokens, segments, attn_gain, w_query, w_keyval, sink_logits, w_out):
    dp_index = lax.axis_index("dp")
    cos_table, sin_table = rope_tables(dp_index)
    pad_rows = ((0, KPAD - KPART), (0, 0))
    w_in = jnp.pad(jnp.concatenate([w_query, w_keyval], axis=1), pad_rows)
    w_back = jnp.pad(w_out.T, pad_rows)
    vmem = pl.BlockSpec(memory_space=pltpu.VMEM)
    width = QCOLS + KVCOLS
    bf16, f32 = jnp.bfloat16, jnp.float32
    dma = pltpu.SemaphoreType.DMA
    return pl.pallas_call(
        attention_kernel,
        out_shape=jax.ShapeDtypeStruct((ROWS, D), bf16),
        in_specs=[vmem] * 7 + [pl.BlockSpec(memory_space=pltpu.SMEM)],
        out_specs=vmem,
        scratch_shapes=[
            pltpu.VMEM((ROWS, D), f32),
            pltpu.VMEM((ROWS, NX * QUART), f32),
            pltpu.VMEM((NX, ROWS, QUART), bf16),
            pltpu.VMEM((NX * NI, ROWS, QUART), bf16),
            pltpu.VMEM((NZ, KPAD, width), bf16),
            pltpu.VMEM((NZ, KPAD, QCOLS), bf16),
            pltpu.VMEM((NX, GROUP, width), f32),
            pltpu.VMEM((NX, GROUP, width), bf16),
            pltpu.VMEM((NX - 1, GROUP, width), bf16),
            pltpu.VMEM((NX, GROUP, 128), f32),
            pltpu.VMEM((3, GROUP, KVCOLS + 128), bf16),
            pltpu.VMEM((NX, GROUP, QCOLS), bf16),
            pltpu.VMEM((NX * NI, ROWS, QUART), bf16),
            pltpu.VMEM((NX * NI, ROWS, QUART), bf16),
            dma((4, 8)),
            dma((4, 8)),
            dma((NX * NI,)),
            dma((NX * NI,)),
            dma((NX - 1,)),
            dma((NX - 1,)),
            dma((2,)),
            dma((2,)),
            dma((NX - 1,)),
            dma((NX - 1,)),
            dma((NX * NI,)),
            dma((NX * NI,)),
        ],
        compiler_params=pltpu.CompilerParams(
            collective_id=0, has_side_effects=True, vmem_limit_bytes=48 * 2**20
        ),
        name="attention",
    )(
        tokens,
        attn_gain.reshape(1, D),
        segments.astype(f32).reshape(ROWS, 1),
        w_in,
        w_back,
        cos_table,
        sin_table,
        sink_logits,
    )


def from_partner(value, axis, apart):
    mask = 2**apart
    pairs = [(source, source ^ mask) for source in range(lax.axis_size(axis))]
    return lax.ppermute(value, axis, pairs)


def rms_scale(row_block, gain_vector):
    values = row_block.astype(jnp.float32)
    mean_square = jnp.mean(values * values, axis=-1, keepdims=True)
    return (values * lax.rsqrt(mean_square + EPSILON) * gain_vector).astype(jnp.bfloat16)


def slot_numbers(route_block, expert_count):
    flat_routes = route_block.reshape(-1)
    onehot = (flat_routes[:, None] == jnp.arange(expert_count, dtype=jnp.int32)[None, :]).astype(
        jnp.int32
    )
    earlier = jnp.cumsum(onehot, axis=0) - onehot
    return jnp.sum(earlier * onehot, axis=1).reshape(route_block.shape)


def route_mix(moe_rows, w_router, route_block):
    expert_count = w_router.shape[1]
    logits = jnp.dot(moe_rows, w_router, preferred_element_type=jnp.float32)
    matches = route_block[:, :, None] == jnp.arange(expert_count, dtype=jnp.int32)[None, None, :]
    chosen = jnp.sum(jnp.where(matches, logits[:, None, :], 0.0), axis=-1)
    return (jax.nn.softmax(chosen, axis=-1), matches)


def send_table(targets, length):
    columns = jnp.arange(length, dtype=jnp.int32)
    return jnp.any(columns[:, None, None] == targets[None, :, :], axis=-1).astype(jnp.bfloat16)


def spread_rows(table, row_block, dp_count):
    placed = jnp.dot(table, row_block, preferred_element_type=jnp.float32)
    return placed.astype(jnp.bfloat16).reshape(dp_count, -1, row_block.shape[1])


def join_rows(returned):
    dp_count, span, width = returned.shape
    return returned.reshape(-1, width)


def pick_rows(returned, targets, weights):
    taken = jnp.take(returned, targets, axis=0).astype(jnp.float32)
    return jnp.sum(weights[:, :, None] * taken, axis=1)


def activate(gate_up):
    gate_part = jnp.minimum(gate_up[:, 0::2], CLAMP_LIMIT)
    up_part = jnp.clip(gate_up[:, 1::2], -CLAMP_LIMIT, CLAMP_LIMIT)
    return ((up_part + 1.0) * gate_part * jax.nn.sigmoid(GLU_SLOPE * gate_part)).astype(
        jnp.bfloat16
    )


def per_device(
    tokens,
    segments,
    attn_gain,
    w_query,
    w_keyval,
    sink_logits,
    w_out,
    moe_gain,
    w_router,
    routes,
    w_gate_up,
    b_gate_up,
    w_down,
    b_down,
):
    tok_rows, model_width = tokens.shape
    dp_count = lax.axis_size("dp")
    dp_index = lax.axis_index("dp")
    inner_index = lax.axis_index("inner")
    residual = attention_layer(
        tokens, segments, attn_gain, w_query, w_keyval, sink_logits, w_out
    )
    moe_in = rms_scale(residual, moe_gain)
    expert_count = w_router.shape[1]
    capacity = 16 * tok_rows // dp_count
    half_cap = capacity // 2
    parity = dp_index % 2
    expert_id = dp_index // 2
    half_rows = w_gate_up.shape[0]
    bias_row = lax.dynamic_slice_in_dim(b_gate_up, expert_id, 1, 0)
    gate_other, down_other = from_partner((w_gate_up, w_down), "dp", 0)
    mix, matches = route_mix(moe_in, w_router, routes)
    expert_mix = jnp.sum(jnp.where(matches, mix[:, :, None], 0.0), axis=1)
    bias_term = jnp.dot(expert_mix, b_down, precision=lax.Precision.HIGHEST)
    slot_index = slot_numbers(routes, expert_count)
    source_flip = (dp_index + inner_index) % 2
    slot_half = (slot_index // half_cap + source_flip) % 2
    targets = routes * capacity + slot_half * half_cap + slot_index % half_cap
    length = expert_count * capacity
    outgoing = spread_rows(send_table(targets, length), moe_in, dp_count)
    received = lax.all_to_all(outgoing, "dp", split_axis=0, concat_axis=0, tiled=True)
    expert_rows = lax.all_gather(received, "inner", axis=0, tiled=True)
    row_block = expert_rows.reshape(-1, expert_rows.shape[-1])
    own_cols = lax.dynamic_slice_in_dim(row_block, parity * half_rows, half_rows, 1)
    other_cols = lax.dynamic_slice_in_dim(row_block, (1 - parity) * half_rows, half_rows, 1)
    own_part = jnp.dot(own_cols, w_gate_up, preferred_element_type=jnp.float32).astype(jnp.bfloat16)
    other_part = jnp.dot(other_cols, gate_other, preferred_element_type=jnp.float32).astype(
        jnp.bfloat16
    )
    own_part, other_part = lax.optimization_barrier((own_part, other_part))
    hidden = activate(own_part.astype(jnp.float32) + other_part.astype(jnp.float32) + bias_row)
    own_out = jnp.dot(hidden, w_down, preferred_element_type=jnp.float32)
    other_out = jnp.dot(hidden, down_other, preferred_element_type=jnp.float32)
    joined = jnp.where(
        parity == 0,
        jnp.concatenate([own_out, other_out], axis=1),
        jnp.concatenate([other_out, own_out], axis=1),
    )
    partial_value = joined.astype(jnp.bfloat16)
    summed = lax.psum_scatter(partial_value, "inner", scatter_dimension=0, tiled=True).astype(
        jnp.float32
    )
    returned = lax.all_to_all(
        summed.reshape(dp_count, -1, summed.shape[-1]).astype(jnp.bfloat16),
        "dp",
        split_axis=0,
        concat_axis=0,
        tiled=True,
    ).astype(jnp.float32)
    moe_sum = pick_rows(join_rows(returned), targets, mix)
    return (residual.astype(jnp.float32) + moe_sum + bias_term).astype(jnp.bfloat16)


def solution(mesh):
    return jax.shard_map(
        per_device,
        mesh=mesh,
        in_specs=(
            P(("dp", "inner"), None),
            P(("dp", "inner")),
            P(),
            P("dp", "inner"),
            P("dp", "inner"),
            P("inner"),
            P("inner", "dp"),
            P(),
            P(),
            P(("dp", "inner"), None),
            P("dp", "inner"),
            P(None, "inner"),
            P("inner", "dp"),
            P(),
        ),
        out_specs=P(("dp", "inner"), None),
        check_vma=False,
    )
```

```python
import functools
import jax
import jax.numpy as jnp
from jax import lax
from jax.experimental import pallas as pl
from jax.experimental.pallas import tpu as pltpu
from jax.sharding import PartitionSpec as P

HEAD_DIM = 64
WINDOW = 128
MESH = pl.DeviceIdType.MESH

EPSILON = 1e-05
ROPE_BASE = 150000.0
CLAMP_LIMIT = 7.0
GLU_SLOPE = 1.702

NX = 4
NZ = 16
NI = 8
NDP = NX * NZ
ROWS = 8
GROUP = ROWS * NI
KPART = 45
KPAD = 48
QUART = NZ * KPAD
HEADS_HERE = 8
QCOLS = HEADS_HERE * HEAD_DIM
KVCOLS = 2 * HEAD_DIM
D = NX * NZ * KPART
HALF = D // 2
HPAD = 1536
TAIL = 1408
TABLE = HALF - TAIL
EXPERTS = 32
SLOTS = 2 * NX * NZ
UNITS = 360
UPAD = 384
NY = 4


def layer_kernel(
    tok_ref,
    gain_ref,
    seg_ref,
    wqkv_ref,
    wout_ref,
    cos_ref,
    sin_ref,
    sink_ref,
    moe_gain_ref,
    routes_ref,
    router_hbm,
    gate_hbm,
    gate_bias_hbm,
    down_hbm,
    down_bias_hbm,
    out_ref,
    norm,
    wide,
    quarter,
    rows_in,
    wq_all,
    wo_all,
    part_f,
    part_out,
    part_in,
    seg_f,
    keyval,
    attended,
    out_part,
    out_in,
    ring_send,
    ring_recv,
    row_send,
    row_recv,
    part_send,
    part_recv,
    key_send,
    key_recv,
    att_send,
    att_recv,
    out_send,
    out_recv,
    res,
    router,
    gate_raw,
    gate_w,
    gate_bias,
    down_w,
    down_bias,
    load_sem,
    halves,
    pay,
    gathered,
    picked,
    rows_all,
    gate_own,
    gate_in,
    hidden,
    sib_out,
    sib_in,
    pair_out,
    pair_in,
    sum_own,
    back_out,
    back_in,
    mixed_out,
    mixed_in,
    z_send,
    z_recv,
    x_send,
    x_recv,
    y_send,
    y_recv,
    sib_send,
    sib_recv,
    gate_send,
    gate_recv,
    hid_send,
    hid_recv,
    fold_send,
    fold_recv,
    pair_send,
    pair_recv,
    back_send,
    back_recv,
    mix_send,
    mix_recv,
):
    dp = lax.axis_index("dp")
    inner = lax.axis_index("inner")
    x = dp // NZ
    z = dp % NZ
    right = x * NZ + (z + 1) % NZ
    left = x * NZ + (z + NZ - 1) % NZ

    barrier = pltpu.get_barrier_semaphore()

    def greet(index, carry):
        other_dp = ((x + index // NI) % NX) * NZ + z
        other_in = (inner + index % NI) % NI
        pl.semaphore_signal(barrier, inc=1, device_id=(other_dp, other_in), device_id_type=MESH)
        return carry

    lax.fori_loop(1, NX * NI, greet, 0)

    def greet_z(index, carry):
        other = x * NZ + (z + index) % NZ
        pl.semaphore_signal(barrier, inc=1, device_id=(other, inner), device_id_type=MESH)
        return carry

    lax.fori_loop(1, NZ, greet_z, 0)
    for other in (
        (dp + 1) % NDP,
        (dp + NDP - 1) % NDP,
        (dp + 2) % NDP,
        (dp + NDP - 2) % NDP,
    ):
        pl.semaphore_signal(barrier, inc=1, device_id=(other, inner), device_id_type=MESH)

    loads = [
        pltpu.make_async_copy(source, target, load_sem.at[number])
        for number, (source, target) in enumerate(
            (
                (router_hbm, router),
                (gate_hbm, gate_raw),
                (gate_bias_hbm, gate_bias),
                (down_hbm, down_w),
                (down_bias_hbm, down_bias),
            )
        )
    ]
    for load in loads:
        load.start()
    wq_all[z] = wqkv_ref[...]
    wo_all[z] = wout_ref[...]
    pl.semaphore_wait(barrier, NX * NI - 1 + NZ - 1 + 4)

    def ring(buffer, lane, step, towards, to):
        owner = (z + NZ - towards * (step - 1)) % NZ
        return pltpu.make_async_remote_copy(
            src_ref=buffer.at[owner],
            dst_ref=buffer.at[owner],
            send_sem=ring_send.at[lane, step - 1],
            recv_sem=ring_recv.at[lane, step - 1],
            device_id=(to, inner),
            device_id_type=MESH,
        )

    lanes = (
        (wq_all, 0, 1, right, 8),
        (wq_all, 1, -1, left, 7),
        (wo_all, 2, 1, right, 7),
        (wo_all, 3, -1, left, 8),
    )
    for buffer, lane, towards, to, last in lanes:
        ring(buffer, lane, 1, towards, to).start()

    values = tok_ref[...].astype(jnp.float32)
    mean_square = jnp.mean(values * values, axis=-1, keepdims=True)
    norm[...] = values * lax.rsqrt(mean_square + EPSILON) * gain_ref[...]
    wide[...] = jnp.zeros_like(wide)
    for block in range(NX * NZ):
        wide[:, block * KPAD : block * KPAD + KPART] = norm[:, block * KPART : (block + 1) * KPART]
    for part in range(NX):
        wide[:, part * QUART + KPART : part * QUART + KPART + 1] = seg_ref[...]
    for part in range(NX):
        quarter[part] = wide[:, part * QUART : (part + 1) * QUART].astype(jnp.bfloat16)

    def row_copy(index):
        other_x = (x + index // NI) % NX
        other_in = (inner + index % NI) % NI
        return pltpu.make_async_remote_copy(
            src_ref=quarter.at[other_x],
            dst_ref=rows_in.at[x * NI + inner],
            send_sem=row_send.at[index],
            recv_sem=row_recv.at[index],
            device_id=(other_x * NZ + z, other_in),
            device_id_type=MESH,
        )

    def start_row(index, carry):
        row_copy(index).start()
        return carry

    lax.fori_loop(1, NX * NI, start_row, 0)
    rows_in[x * NI + inner] = quarter[x]

    for step in range(1, 9):
        for buffer, lane, towards, to, last in lanes:
            if step <= last:
                ring(buffer, lane, step, towards, to).wait_recv()
            if step + 1 <= last:
                ring(buffer, lane, step + 1, towards, to).start()

    def wait_row(index, carry):
        row_copy(index).wait_recv()
        return carry

    lax.fori_loop(1, NX * NI, wait_row, 0)

    all_rows = rows_in[...].astype(jnp.float32).reshape(NX * GROUP, QUART)
    seg_f[...] = all_rows[:, :128].reshape(NX, GROUP, 128)
    product = jnp.dot(
        all_rows.astype(jnp.bfloat16),
        wq_all[...].reshape(QUART, QCOLS + KVCOLS),
        preferred_element_type=jnp.float32,
    ).reshape(NX, GROUP, QCOLS + KVCOLS)
    part_f[...] = product
    part_out[...] = product.astype(jnp.bfloat16)

    def part_copy(ahead):
        other = (x + ahead) % NX
        return pltpu.make_async_remote_copy(
            src_ref=part_out.at[other],
            dst_ref=part_in.at[ahead - 1],
            send_sem=part_send.at[ahead - 1],
            recv_sem=part_recv.at[ahead - 1],
            device_id=(other * NZ + z, inner),
            device_id_type=MESH,
        )

    for ahead in range(1, NX):
        part_copy(ahead).start()
    total = part_f[x]
    for ahead in range(1, NX):
        part_copy(ahead).wait_recv()
        total = total + part_in[ahead - 1].astype(jnp.float32)

    width = QCOLS + KVCOLS
    cosine = jnp.concatenate([cos_ref[:, :128]] * 4 + [cos_ref[:, 128:]], axis=1)
    sine = jnp.concatenate([sin_ref[:, :128]] * 4 + [sin_ref[:, 128:]], axis=1)
    column = lax.broadcasted_iota(jnp.int32, (GROUP, width), 1)
    swapped = jnp.where(
        column % HEAD_DIM < HEAD_DIM // 2,
        pltpu.roll(total, width - HEAD_DIM // 2, 1),
        pltpu.roll(total, HEAD_DIM // 2, 1),
    )
    turned = (total * cosine + swapped * sine).astype(jnp.bfloat16)
    own_seg = seg_f[x][:, KPART : KPART + 1]
    keyval[2, :, :KVCOLS] = turned[:, QCOLS:]
    keyval[2, :, KVCOLS:] = jnp.broadcast_to(own_seg, (GROUP, 128)).astype(jnp.bfloat16)

    def key_copy(ahead):
        return pltpu.make_async_remote_copy(
            src_ref=keyval.at[2],
            dst_ref=keyval.at[2 - ahead],
            send_sem=key_send.at[ahead - 1],
            recv_sem=key_recv.at[ahead - 1],
            device_id=((dp + ahead) % NDP, inner),
            device_id_type=MESH,
        )

    for ahead in (1, 2):
        key_copy(ahead).start()
    for ahead in (1, 2):
        key_copy(ahead).wait_recv()

    count = 3 * GROUP
    window = keyval[...].reshape(count, KVCOLS + 128)
    key_block = window[:, :HEAD_DIM]
    value_block = window[:, HEAD_DIM:KVCOLS]
    nt = (((1,), (1,)), ((), ()))
    key_seg = lax.dot_general(
        jnp.ones((GROUP, 128), jnp.bfloat16),
        window[:, KVCOLS:],
        nt,
        preferred_element_type=jnp.float32,
    )
    row = lax.broadcasted_iota(jnp.int32, (GROUP, count), 0)
    key = lax.broadcasted_iota(jnp.int32, (GROUP, count), 1)
    distance = row + 2 * GROUP - key
    allowed = (
        (distance >= 0)
        & (distance < WINDOW)
        & (key + (dp - 2) * GROUP >= 0)
        & (key_seg == own_seg * 128.0)
    )
    for head in range(HEADS_HERE):
        scores = lax.dot_general(
            turned[:, head * HEAD_DIM : (head + 1) * HEAD_DIM],
            key_block,
            nt,
            preferred_element_type=jnp.float32,
        ) * HEAD_DIM ** (-0.5)
        scores = jnp.where(allowed, scores, -1e30)
        sink = sink_ref[head]
        row_max = jnp.maximum(jnp.max(scores, axis=-1, keepdims=True), sink)
        weights = jnp.exp(scores - row_max)
        denominator = jnp.sum(weights, axis=-1, keepdims=True) + jnp.exp(sink - row_max)
        probabilities = (weights / denominator).astype(jnp.bfloat16)
        mixed = jnp.dot(probabilities, value_block, preferred_element_type=jnp.float32)
        attended[x, :, head * HEAD_DIM : (head + 1) * HEAD_DIM] = mixed.astype(jnp.bfloat16)

    def att_copy(ahead):
        return pltpu.make_async_remote_copy(
            src_ref=attended.at[x],
            dst_ref=attended.at[x],
            send_sem=att_send.at[ahead - 1],
            recv_sem=att_recv.at[ahead - 1],
            device_id=(((x + ahead) % NX) * NZ + z, inner),
            device_id_type=MESH,
        )

    for ahead in range(1, NX):
        att_copy(ahead).start()
    for ahead in range(1, NX):
        att_copy(ahead).wait_recv()
    projected = lax.dot_general(
        attended[...].reshape(NX * GROUP, QCOLS),
        wo_all[...].reshape(QUART, QCOLS),
        nt,
        preferred_element_type=jnp.float32,
    )
    out_part[...] = projected.reshape(NX * NI, ROWS, QUART).astype(jnp.bfloat16)

    def out_copy(index):
        other_x = (x + index // NI) % NX
        other_in = (inner + index % NI) % NI
        return pltpu.make_async_remote_copy(
            src_ref=out_part.at[other_x * NI + other_in],
            dst_ref=out_in.at[x * NI + inner],
            send_sem=out_send.at[index],
            recv_sem=out_recv.at[index],
            device_id=(other_x * NZ + z, other_in),
            device_id_type=MESH,
        )

    def start_out(index, carry):
        out_copy(index).start()
        return carry

    def wait_out(index, carry):
        out_copy(index).wait_recv()
        return carry

    lax.fori_loop(1, NX * NI, start_out, 0)
    out_in[x * NI + inner] = out_part[x * NI + inner]
    lax.fori_loop(1, NX * NI, wait_out, 0)
    summed = jnp.sum(
        out_in[...].astype(jnp.float32).reshape(NX, NI, ROWS, QUART), axis=1
    )
    for part in range(NX):
        wide[:, part * QUART : (part + 1) * QUART] = summed[part]
    for block in range(NX * NZ):
        norm[:, block * KPART : (block + 1) * KPART] = wide[:, block * KPAD : block * KPAD + KPART]
    res[...] = (tok_ref[...].astype(jnp.float32) + norm[...]).astype(jnp.bfloat16)

    bf16, f32 = jnp.bfloat16, jnp.float32
    nn = (((1,), (0,)), ((), ()))

    def iota(shape, dimension):
        return lax.broadcasted_iota(jnp.int32, shape, dimension)

    def ones_where(condition):
        return jnp.where(condition, 1.0, 0.0)

    half = z % 2
    chip_y = inner // 2
    core = inner % 2
    partner = x * NZ + z + 1 - 2 * half
    sibling = inner + 1 - 2 * core
    for load in loads:
        load.wait()

    values = res[...].astype(f32)
    mean_square = jnp.mean(values * values, axis=-1, keepdims=True)
    moe_in = (values * lax.rsqrt(mean_square + EPSILON) * moe_gain_ref[...]).astype(bf16)
    norm[...] = moe_in.astype(f32)
    halves[...] = jnp.zeros_like(halves)
    for part in range(2):
        halves[part, :, :HALF] = norm[:, part * HALF : (part + 1) * HALF]

    logits = jnp.dot(moe_in, router[...], preferred_element_type=f32)
    expert = iota((ROWS, EXPERTS), 1)
    named = [ones_where(routes_ref[:, k : k + 1] == expert) for k in range(4)]
    chosen = [jnp.sum(match * logits, axis=-1, keepdims=True) for match in named]
    largest = jnp.maximum(jnp.maximum(chosen[0], chosen[1]), jnp.maximum(chosen[2], chosen[3]))
    raised = [jnp.exp(value - largest) for value in chosen]
    whole = raised[0] + raised[1] + raised[2] + raised[3]
    onehot = named[0] + named[1] + named[2] + named[3]
    mix = (
        named[0] * raised[0] + named[1] * raised[1] + named[2] * raised[2] + named[3] * raised[3]
    ) / whole
    earlier = jnp.dot(
        ones_where(iota((ROWS, ROWS), 0) > iota((ROWS, ROWS), 1)),
        onehot,
        preferred_element_type=f32,
    )
    mix_high = mix.astype(bf16).astype(f32)
    mix_low = mix - mix_high
    column = iota((EXPERTS, 8 * 128), 1)
    source = iota((EXPERTS, 8 * 128), 0)
    table = jnp.zeros((ROWS, 8 * 128), f32)
    for slot in range(2):
        here = onehot * ones_where(earlier == slot)
        for kind, value in enumerate((here, here * mix_high, here * mix_low)):
            place = (source % 8) * 128 + TABLE + kind * 8 + (source // 8) * 2 + slot
            table = table + jnp.dot(
                value.astype(bf16),
                ones_where(column == place).astype(bf16),
                preferred_element_type=f32,
            )
    for other in range(NZ):
        part = other % 2
        pair = other // 2
        pay[other, :, :TAIL] = halves[part, :, :TAIL].astype(bf16)
        pay[other, :, TAIL:] = (
            halves[part, :, TAIL:] + table[:, pair * 128 : (pair + 1) * 128]
        ).astype(bf16)

    def z_copy(index):
        other = (z + index) % NZ
        return pltpu.make_async_remote_copy(
            src_ref=pay.at[other],
            dst_ref=gathered.at[z],
            send_sem=z_send.at[index],
            recv_sem=z_recv.at[index],
            device_id=(x * NZ + other, inner),
            device_id_type=MESH,
        )

    def start_z(index, carry):
        z_copy(index).start()
        return carry

    def wait_z(index, carry):
        z_copy(index).wait_recv()
        return carry

    lax.fori_loop(1, NZ, start_z, 0)
    gathered[z] = pay[z]

    bias_term = jnp.dot(mix, down_bias[...], precision=lax.Precision.HIGHEST)
    target = iota((2 * UNITS, 2 * UPAD), 1)
    place = iota((2 * UNITS, 2 * UPAD), 0)
    unweave = ones_where(target == place // 2 + (place % 2) * UPAD).astype(bf16)

    def sort_columns(index, carry):
        lines = pl.ds(pl.multiple_of(index * 144, 16), 144)
        gate_w[lines, :] = jnp.dot(gate_raw[lines, :], unweave, preferred_element_type=f32).astype(
            bf16
        )
        return carry

    lax.fori_loop(0, HALF // 144, sort_columns, 0)
    bias_row = gate_bias[pl.ds(dp // 2, 1), :]
    bias_high = bias_row.astype(bf16).astype(f32)
    bias_mid = (bias_row - bias_high).astype(bf16).astype(f32)
    bias_low = bias_row - bias_high - bias_mid
    line = iota((ROWS, 2 * UNITS), 0)
    bias_parts = jnp.where(
        line == 0, bias_high, jnp.where(line == 1, bias_mid, jnp.where(line == 2, bias_low, 0.0))
    )
    bias = jnp.sum(
        jnp.dot(bias_parts.astype(bf16), unweave, preferred_element_type=f32),
        axis=0,
        keepdims=True,
    )

    lax.fori_loop(1, NZ, wait_z, 0)
    row_total = NZ * ROWS
    near = gathered[...].astype(f32).reshape(row_total, HPAD)
    near_tail = near[:, TAIL:].astype(bf16)
    slot_row = iota((SLOTS, 128), 0)
    slot_lane = iota((SLOTS, 128), 1)
    select = lax.dot_general(
        ones_where(slot_lane - TABLE == slot_row // NZ).astype(bf16),
        near_tail,
        nt,
        preferred_element_type=f32,
    ) * ones_where(slot_row % NZ == slot_lane // ROWS)
    chosen_rows = jnp.dot(
        select.astype(bf16), near[:, :HALF].astype(bf16), preferred_element_type=f32
    )
    picked[...] = chosen_rows.astype(bf16).reshape(NX, 2 * NZ, HALF)

    def mix_matrix(kind):
        spread = jnp.dot(
            near_tail,
            ones_where(slot_row - TABLE - kind * 8 == slot_lane // NZ).astype(bf16),
            preferred_element_type=f32,
        )
        return (spread * ones_where(slot_row // ROWS == slot_lane % NZ)).astype(bf16)

    def x_copy(ahead):
        other = (x + ahead) % NX
        return pltpu.make_async_remote_copy(
            src_ref=picked.at[other],
            dst_ref=rows_all.at[inner, x],
            send_sem=x_send.at[ahead],
            recv_sem=x_recv.at[ahead],
            device_id=(other * NZ + z, inner),
            device_id_type=MESH,
        )

    def y_copy(ahead, back):
        block = rows_all.at[inner, (x + NX - back) % NX]
        return pltpu.make_async_remote_copy(
            src_ref=block,
            dst_ref=block,
            send_sem=y_send.at[ahead, back],
            recv_sem=y_recv.at[ahead, back],
            device_id=(dp, ((chip_y + ahead) % NY) * 2 + core),
            device_id_type=MESH,
        )

    def sib_copy(turn, chip):
        chunk = rows_all.at[chip * 2 + core]
        return pltpu.make_async_remote_copy(
            src_ref=chunk,
            dst_ref=chunk,
            send_sem=sib_send.at[turn],
            recv_sem=sib_recv.at[turn],
            device_id=(dp, sibling),
            device_id_type=MESH,
        )

    for ahead in range(1, NX):
        x_copy(ahead).start()
    rows_all[inner, x] = picked[x]
    for back in range(NX):
        if back:
            x_copy(back).wait_recv()
        for ahead in (1, 3, 2):
            y_copy(ahead, back).start()
    sib_copy(0, chip_y).start()

    def gate_copy(chunk):
        return pltpu.make_async_remote_copy(
            src_ref=gate_own.at[chunk, 1 - half],
            dst_ref=gate_in.at[chunk],
            send_sem=gate_send.at[chunk],
            recv_sem=gate_recv.at[chunk],
            device_id=(partner, inner),
            device_id_type=MESH,
        )

    def hid_copy(chunk):
        return pltpu.make_async_remote_copy(
            src_ref=hidden.at[chunk, half],
            dst_ref=hidden.at[chunk, half],
            send_sem=hid_send.at[chunk],
            recv_sem=hid_recv.at[chunk],
            device_id=(partner, inner),
            device_id_type=MESH,
        )

    def fold_copy(turn):
        return pltpu.make_async_remote_copy(
            src_ref=sib_out.at[turn],
            dst_ref=sib_in.at[turn],
            send_sem=fold_send.at[turn],
            recv_sem=fold_recv.at[turn],
            device_id=(dp, sibling),
            device_id_type=MESH,
        )

    def pair_copy(turn, back):
        return pltpu.make_async_remote_copy(
            src_ref=pair_out.at[turn],
            dst_ref=pair_in.at[turn],
            send_sem=pair_send.at[turn],
            recv_sem=pair_recv.at[turn],
            device_id=(dp, ((chip_y + NY - back) % NY) * 2 + core),
            device_id_type=MESH,
        )

    def project(chunk):
        rows = rows_all[chunk].reshape(SLOTS, HALF)
        gate_own[chunk] = (
            jnp.dot(rows, gate_w[...], preferred_element_type=f32)
            .astype(bf16)
            .reshape(2, SLOTS // 2, 2 * UPAD)
        )
        gate_copy(chunk).start()

    def activate(chunk):
        gate_copy(chunk).wait_recv()
        gate_up = gate_own[chunk, half].astype(f32) + gate_in[chunk].astype(f32) + bias
        gate = jnp.minimum(gate_up[:, :UPAD], CLAMP_LIMIT)
        up = jnp.clip(gate_up[:, UPAD:], -CLAMP_LIMIT, CLAMP_LIMIT)
        hidden[chunk, half] = ((up + 1.0) * gate * jax.nn.sigmoid(GLU_SLOPE * gate)).astype(bf16)
        hid_copy(chunk).start()

    def lower(chunk):
        pl_wait = pltpu.make_async_remote_copy(
            src_ref=hidden.at[chunk, 1 - half],
            dst_ref=hidden.at[chunk, 1 - half],
            send_sem=hid_send.at[chunk],
            recv_sem=hid_recv.at[chunk],
            device_id=(partner, inner),
            device_id_type=MESH,
        )
        pl_wait.wait_recv()
        units = hidden[chunk].reshape(SLOTS, UPAD)[:, :UNITS]
        return jnp.dot(units, down_w[...], preferred_element_type=f32).astype(bf16)

    def turn_of(turn):
        back = (turn * (turn + 1) // 2) % NY
        return back, (chip_y + NY - back) % NY

    def step(turn, carry):
        @pl.when(turn < NY)
        def _():
            back, chip = turn_of(turn)

            @pl.when(turn > 0)
            def _():
                for block in range(NX):
                    y_copy(back, block).wait_recv()
                sib_copy(turn, chip).start()

            project(chip * 2 + core)
            sib_copy(turn, chip).wait_recv()
            project(chip * 2 + 1 - core)

        @pl.when((turn >= 1) & (turn < NY + 1))
        def _():
            back, chip = turn_of(turn - 1)
            activate(chip * 2 + core)
            activate(chip * 2 + 1 - core)

        @pl.when(turn >= 2)
        def _():
            now = turn - 2
            back, chip = turn_of(now)
            sib_out[now] = lower(chip * 2 + 1 - core)
            fold_copy(now).start()
            kept = lower(chip * 2 + core).astype(f32)
            fold_copy(now).wait_recv()
            kept = kept + sib_in[now].astype(f32)

            @pl.when(now == 0)
            def _():
                sum_own[...] = kept

            @pl.when(now > 0)
            def _():
                pair_out[now] = kept.astype(bf16)
                pair_copy(now, back).start()

        return carry

    lax.fori_loop(0, NY + 2, step, 0)

    total = sum_own[...]
    for turn in range(1, NY):
        pair_copy(turn, (turn * (turn + 1) // 2) % NY).wait_recv()
        total = total + pair_in[turn].astype(f32)
    back_out[...] = total.astype(bf16).reshape(NX, 2 * NZ, HALF)

    def back_copy(ahead):
        other = (x + ahead) % NX
        return pltpu.make_async_remote_copy(
            src_ref=back_out.at[other],
            dst_ref=back_in.at[x],
            send_sem=back_send.at[ahead],
            recv_sem=back_recv.at[ahead],
            device_id=(other * NZ + z, inner),
            device_id_type=MESH,
        )

    for ahead in range(1, NX):
        back_copy(ahead).start()
    back_in[x] = back_out[x]
    for ahead in range(1, NX):
        back_copy(ahead).wait_recv()
    answers = back_in[...].reshape(SLOTS, HALF)
    combined = jnp.dot(mix_matrix(1), answers, preferred_element_type=f32) + jnp.dot(
        mix_matrix(2), answers, preferred_element_type=f32
    )
    mixed_out[...] = combined.reshape(NZ, ROWS, HALF).astype(bf16)

    def mix_copy(index):
        other = (z + index) % NZ
        return pltpu.make_async_remote_copy(
            src_ref=mixed_out.at[other],
            dst_ref=mixed_in.at[z],
            send_sem=mix_send.at[index],
            recv_sem=mix_recv.at[index],
            device_id=(x * NZ + other, inner),
            device_id_type=MESH,
        )

    def start_mix(index, carry):
        mix_copy(index).start()
        return carry

    def wait_mix(index, carry):
        mix_copy(index).wait_recv()
        return carry

    lax.fori_loop(1, NZ, start_mix, 0)
    mixed_in[z] = mixed_out[z]
    lax.fori_loop(1, NZ, wait_mix, 0)
    both = jnp.sum(mixed_in[...].astype(f32).reshape(NZ // 2, 2, ROWS, HALF), axis=0)
    for part in range(2):
        norm[:, part * HALF : (part + 1) * HALF] = both[part]
    out_ref[...] = (res[...].astype(f32) + norm[...] + bias_term).astype(bf16)


    for buffer, lane, towards, to, last in lanes:
        for step in range(1, last + 1):
            ring(buffer, lane, step, towards, to).wait_send()

    def wait_sends(index, carry):
        row_copy(index).wait_send()
        out_copy(index).wait_send()
        return carry

    lax.fori_loop(1, NX * NI, wait_sends, 0)
    for ahead in range(1, NX):
        part_copy(ahead).wait_send()
        att_copy(ahead).wait_send()
    for ahead in (1, 2):
        key_copy(ahead).wait_send()

    def wait_z_sends(index, carry):
        z_copy(index).wait_send()
        mix_copy(index).wait_send()
        return carry

    lax.fori_loop(1, NZ, wait_z_sends, 0)
    for ahead in range(1, NX):
        x_copy(ahead).wait_send()
        back_copy(ahead).wait_send()
    for ahead in range(1, NY):
        for block in range(NX):
            y_copy(ahead, block).wait_send()
        pair_copy(ahead, (ahead * (ahead + 1) // 2) % NY).wait_send()

    def wait_turn(turn, carry):
        back, chip = turn_of(turn)
        sib_copy(turn, chip).wait_send()
        fold_copy(turn).wait_send()
        return carry

    def wait_chunk(chunk, carry):
        gate_copy(chunk).wait_send()
        hid_copy(chunk).wait_send()
        return carry

    lax.fori_loop(0, NY, wait_turn, 0)
    lax.fori_loop(0, NI, wait_chunk, 0)


def rope_tables(dp_index):
    half = HEAD_DIM // 2
    frequency = ROPE_BASE ** (-2.0 * jnp.arange(half, dtype=jnp.float32) / HEAD_DIM)
    positions = dp_index * GROUP + jnp.arange(GROUP, dtype=jnp.int32)
    angles = positions.astype(jnp.float32)[:, None] * frequency[None, :]
    cosine = jnp.cos(angles)
    sine = jnp.sin(angles)
    ones = jnp.ones((GROUP, HEAD_DIM), jnp.float32)
    head_cos = jnp.concatenate([cosine, cosine], axis=1)
    head_sin = jnp.concatenate([-sine, sine], axis=1)
    return (
        jnp.concatenate([head_cos, head_cos, head_cos, ones], axis=1),
        jnp.concatenate([head_sin, head_sin, head_sin, 0.0 * ones], axis=1),
    )


def per_device(
    tokens,
    segments,
    attn_gain,
    w_query,
    w_keyval,
    sink_logits,
    w_out,
    moe_gain,
    w_router,
    routes,
    w_gate_up,
    b_gate_up,
    w_down,
    b_down,
):
    dp_index = lax.axis_index("dp")
    cos_table, sin_table = rope_tables(dp_index)
    pad_rows = ((0, KPAD - KPART), (0, 0))
    w_in = jnp.pad(jnp.concatenate([w_query, w_keyval], axis=1), pad_rows)
    w_back = jnp.pad(w_out.T, pad_rows)
    vmem = pl.BlockSpec(memory_space=pltpu.VMEM)
    smem = pl.BlockSpec(memory_space=pltpu.SMEM)
    anywhere = pl.BlockSpec(memory_space=pl.ANY)
    width = QCOLS + KVCOLS
    bf16, f32 = jnp.bfloat16, jnp.float32
    dma = pltpu.SemaphoreType.DMA
    buffers = [
        ((ROWS, D), f32),
        ((ROWS, NX * QUART), f32),
        ((NX, ROWS, QUART), bf16),
        ((NX * NI, ROWS, QUART), bf16),
        ((NZ, KPAD, width), bf16),
        ((NZ, KPAD, QCOLS), bf16),
        ((NX, GROUP, width), f32),
        ((NX, GROUP, width), bf16),
        ((NX - 1, GROUP, width), bf16),
        ((NX, GROUP, 128), f32),
        ((3, GROUP, KVCOLS + 128), bf16),
        ((NX, GROUP, QCOLS), bf16),
        ((NX * NI, ROWS, QUART), bf16),
        ((NX * NI, ROWS, QUART), bf16),
    ]
    semaphores = [(4, 8), (NX * NI,), (NX - 1,), (2,), (NX - 1,), (NX * NI,)]
    expert_inputs = [
        ((ROWS, D), bf16),
        ((D, EXPERTS), bf16),
        ((HALF, 2 * UNITS), bf16),
        ((HALF, 2 * UPAD), bf16),
        ((EXPERTS, 2 * UNITS), f32),
        ((UNITS, HALF), bf16),
        ((EXPERTS, D), f32),
    ]
    expert_buffers = [
        ((2, ROWS, HPAD), f32),
        ((NZ, ROWS, HPAD), bf16),
        ((NZ, ROWS, HPAD), bf16),
        ((NX, 2 * NZ, HALF), bf16),
        ((NI, NX, 2 * NZ, HALF), bf16),
        ((NI, 2, SLOTS // 2, 2 * UPAD), bf16),
        ((NI, SLOTS // 2, 2 * UPAD), bf16),
        ((NI, 2, SLOTS // 2, UPAD), bf16),
        ((NY, SLOTS, HALF), bf16),
        ((NY, SLOTS, HALF), bf16),
        ((NY, SLOTS, HALF), bf16),
        ((NY, SLOTS, HALF), bf16),
        ((SLOTS, HALF), f32),
        ((NX, 2 * NZ, HALF), bf16),
        ((NX, 2 * NZ, HALF), bf16),
        ((NZ, ROWS, HALF), bf16),
        ((NZ, ROWS, HALF), bf16),
    ]
    expert_semaphores = [(NZ,), (NX,), (NY, NX), (NY,), (NI,), (NI,), (NY,), (NY,), (NX,), (NZ,)]

    def allocate(shapes):
        return [pltpu.VMEM(shape, dtype) for shape, dtype in shapes]

    def pairs(shapes):
        return [dma(shape) for shape in shapes for _ in range(2)]

    return pl.pallas_call(
        layer_kernel,
        out_shape=jax.ShapeDtypeStruct((ROWS, D), bf16),
        in_specs=[vmem] * 7 + [smem] + [vmem] * 2 + [anywhere] * 5,
        out_specs=vmem,
        scratch_shapes=allocate(buffers)
        + pairs(semaphores)
        + allocate(expert_inputs)
        + [dma((5,))]
        + allocate(expert_buffers)
        + pairs(expert_semaphores),
        compiler_params=pltpu.CompilerParams(
            collective_id=0, has_side_effects=True, vmem_limit_bytes=56 * 2**20
        ),
        name="layer",
    )(
        tokens,
        attn_gain.reshape(1, D),
        segments.astype(f32).reshape(ROWS, 1),
        w_in,
        w_back,
        cos_table,
        sin_table,
        sink_logits,
        moe_gain.reshape(1, D),
        routes,
        w_router,
        w_gate_up,
        b_gate_up,
        w_down,
        b_down,
    )


def solution(mesh):
    return jax.shard_map(
        per_device,
        mesh=mesh,
        in_specs=(
            P(("dp", "inner"), None),
            P(("dp", "inner")),
            P(),
            P("dp", "inner"),
            P("dp", "inner"),
            P("inner"),
            P("inner", "dp"),
            P(),
            P(),
            P(("dp", "inner"), None),
            P("dp", "inner"),
            P(None, "inner"),
            P("inner", "dp"),
            P(),
        ),
        out_specs=P(("dp", "inner"), None),
        check_vma=False,
    )
```

```python
import functools
import jax
import jax.numpy as jnp
from jax import lax
from jax.experimental import pallas as pl
from jax.experimental.pallas import tpu as pltpu
from jax.sharding import PartitionSpec as P

HEAD_DIM = 64
WINDOW = 128
MESH = pl.DeviceIdType.MESH

EPSILON = 1e-05
ROPE_BASE = 150000.0
CLAMP_LIMIT = 7.0
GLU_SLOPE = 1.702

NX = 4
NZ = 16
NI = 8
NDP = NX * NZ
ROWS = 8
GROUP = ROWS * NI
KPART = 45
KPAD = 48
TEAM = 2 * NX
RING = NZ // 2
QUART = RING * KPAD
HEADS_HERE = 8
QCOLS = HEADS_HERE * HEAD_DIM
KVCOLS = 2 * HEAD_DIM
D = NX * NZ * KPART
HALF = D // 2
HPAD = 1536
TAIL = 1408
TABLE = HALF - TAIL
EXPERTS = 32
SLOTS = 2 * NX * NZ
UNITS = 360
UPAD = 384
NY = 4


def places(block):
    part = 2 * (block // NZ) + block % 2
    return part * QUART + (block % NZ) // 2 * KPAD, block * KPART


def layer_kernel(
    tok_ref,
    gain_ref,
    seg_ref,
    wq_ref,
    wkv_ref,
    wout_ref,
    cos_ref,
    sin_ref,
    sink_ref,
    moe_gain_ref,
    routes_ref,
    router_hbm,
    gate_hbm,
    gate_bias_hbm,
    down_hbm,
    down_bias_hbm,
    out_ref,
    norm,
    wide,
    quarter,
    rows_in,
    wq_all,
    wo_all,
    part_f,
    part_out,
    part_in,
    seg_f,
    keyval,
    attended,
    out_part,
    out_in,
    ring_send,
    ring_recv,
    row_send,
    row_recv,
    part_send,
    part_recv,
    key_send,
    key_recv,
    att_send,
    att_recv,
    out_send,
    out_recv,
    res,
    router,
    gate_raw,
    gate_w,
    gate_bias,
    down_w,
    down_bias,
    load_sem,
    halves,
    pay,
    gathered,
    picked,
    rows_all,
    gate_own,
    gate_in,
    hidden,
    sib_out,
    sib_in,
    pair_out,
    pair_in,
    sum_own,
    back_out,
    back_in,
    mixed_out,
    mixed_in,
    z_send,
    z_recv,
    x_send,
    x_recv,
    y_send,
    y_recv,
    sib_send,
    sib_recv,
    gate_send,
    gate_recv,
    hid_send,
    hid_recv,
    fold_send,
    fold_recv,
    pair_send,
    pair_recv,
    back_send,
    back_recv,
    mix_send,
    mix_recv,
):
    dp = lax.axis_index("dp")
    inner = lax.axis_index("inner")
    x = dp // NZ
    z = dp % NZ
    right = x * NZ + (z + 2) % NZ
    left = x * NZ + (z + NZ - 2) % NZ
    spot = z // 2
    team = 2 * x + z % 2

    def member(ahead):
        other = (team + ahead) % TEAM
        return other, (other // 2) * NZ + 2 * spot + other % 2

    barrier = pltpu.get_barrier_semaphore()

    def greet(index, carry):
        other, other_dp = member(index // NI)
        other_in = (inner + index % NI) % NI
        pl.semaphore_signal(barrier, inc=1, device_id=(other_dp, other_in), device_id_type=MESH)
        return carry

    lax.fori_loop(1, TEAM * NI, greet, 0)

    def greet_z(index, carry):
        other = x * NZ + (z + index) % NZ
        pl.semaphore_signal(barrier, inc=1, device_id=(other, inner), device_id_type=MESH)
        return carry

    lax.fori_loop(1, NZ, greet_z, 0)
    for other in (
        (dp + 1) % NDP,
        (dp + NDP - 1) % NDP,
        (dp + 2) % NDP,
        (dp + NDP - 2) % NDP,
    ):
        pl.semaphore_signal(barrier, inc=1, device_id=(other, inner), device_id_type=MESH)

    loads = [
        pltpu.make_async_copy(source, target, load_sem.at[number])
        for number, (source, target) in enumerate(
            (
                (router_hbm, router),
                (gate_hbm, gate_raw),
                (gate_bias_hbm, gate_bias),
                (down_hbm, down_w),
                (down_bias_hbm, down_bias),
            )
        )
    ]
    for load in loads:
        load.start()
    widen = jnp.where(
        lax.broadcasted_iota(jnp.int32, (KPAD, KPART), 0)
        == lax.broadcasted_iota(jnp.int32, (KPAD, KPART), 1),
        1.0,
        0.0,
    ).astype(jnp.bfloat16)
    for source, target, low, high in (
        (wq_ref, wq_all, 0, QCOLS),
        (wkv_ref, wq_all, QCOLS, QCOLS + KVCOLS),
        (wout_ref, wo_all, 0, QCOLS),
    ):
        target[spot, :, low:high] = jnp.dot(
            widen, source[...], preferred_element_type=jnp.float32
        ).astype(jnp.bfloat16)
    pl.semaphore_wait(barrier, TEAM * NI - 1 + NZ - 1 + 4)

    def ring(buffer, lane, step, towards, to):
        owner = (spot + RING - towards * (step - 1)) % RING
        return pltpu.make_async_remote_copy(
            src_ref=buffer.at[owner],
            dst_ref=buffer.at[owner],
            send_sem=ring_send.at[lane, step - 1],
            recv_sem=ring_recv.at[lane, step - 1],
            device_id=(to, inner),
            device_id_type=MESH,
        )

    lanes = (
        (wq_all, 0, 1, right, 4),
        (wq_all, 1, -1, left, 3),
        (wo_all, 2, 1, right, 3),
        (wo_all, 3, -1, left, 4),
    )
    for buffer, lane, towards, to, last in lanes:
        ring(buffer, lane, 1, towards, to).start()

    values = tok_ref[...].astype(jnp.float32)
    mean_square = jnp.mean(values * values, axis=-1, keepdims=True)
    norm[...] = values * lax.rsqrt(mean_square + EPSILON) * gain_ref[...].reshape(1, D)
    wide[...] = jnp.zeros_like(wide)
    for block in range(NX * NZ):
        wide_at, block_at = places(block)
        wide[:, wide_at : wide_at + KPART] = norm[:, block_at : block_at + KPART]
    row_number = lax.broadcasted_iota(jnp.int32, (ROWS, 1), 0)
    own_segments = jnp.zeros((ROWS, 1), jnp.float32)
    for number in range(ROWS):
        own_segments = jnp.where(
            row_number == number, seg_ref[number].astype(jnp.float32), own_segments
        )
    for part in range(TEAM):
        wide[:, part * QUART + KPART : part * QUART + KPART + 1] = own_segments
    for part in range(TEAM):
        quarter[part] = wide[:, part * QUART : (part + 1) * QUART].astype(jnp.bfloat16)

    def row_copy(index):
        other, other_dp = member(index // NI)
        other_in = (inner + index % NI) % NI
        return pltpu.make_async_remote_copy(
            src_ref=quarter.at[other],
            dst_ref=rows_in.at[team * NI + inner],
            send_sem=row_send.at[index],
            recv_sem=row_recv.at[index],
            device_id=(other_dp, other_in),
            device_id_type=MESH,
        )

    def start_row(index, carry):
        row_copy(index).start()
        return carry

    lax.fori_loop(1, TEAM * NI, start_row, 0)
    rows_in[team * NI + inner] = quarter[team]

    for step in range(1, RING // 2 + 1):
        for buffer, lane, towards, to, last in lanes:
            if step <= last:
                ring(buffer, lane, step, towards, to).wait_recv()
            if step + 1 <= last:
                ring(buffer, lane, step + 1, towards, to).start()

    def wait_row(index, carry):
        row_copy(index).wait_recv()
        return carry

    lax.fori_loop(1, TEAM * NI, wait_row, 0)

    all_rows = rows_in[...].astype(jnp.float32).reshape(TEAM * GROUP, QUART)
    seg_f[...] = all_rows[:, :128].reshape(TEAM, GROUP, 128)
    product = jnp.dot(
        all_rows.astype(jnp.bfloat16),
        wq_all[...].reshape(QUART, QCOLS + KVCOLS),
        preferred_element_type=jnp.float32,
    ).reshape(TEAM, GROUP, QCOLS + KVCOLS)
    part_f[...] = product
    part_out[...] = product.astype(jnp.bfloat16)

    def part_copy(ahead):
        other, other_dp = member(ahead)
        return pltpu.make_async_remote_copy(
            src_ref=part_out.at[other],
            dst_ref=part_in.at[ahead - 1],
            send_sem=part_send.at[ahead - 1],
            recv_sem=part_recv.at[ahead - 1],
            device_id=(other_dp, inner),
            device_id_type=MESH,
        )

    for ahead in range(1, TEAM):
        part_copy(ahead).start()
    total = part_f[team]
    for ahead in range(1, TEAM):
        part_copy(ahead).wait_recv()
        total = total + part_in[ahead - 1].astype(jnp.float32)

    width = QCOLS + KVCOLS
    cosine = jnp.concatenate([cos_ref[:, :128]] * 4 + [cos_ref[:, 128:]], axis=1)
    sine = jnp.concatenate([sin_ref[:, :128]] * 4 + [sin_ref[:, 128:]], axis=1)
    column = lax.broadcasted_iota(jnp.int32, (GROUP, width), 1)
    swapped = jnp.where(
        column % HEAD_DIM < HEAD_DIM // 2,
        pltpu.roll(total, width - HEAD_DIM // 2, 1),
        pltpu.roll(total, HEAD_DIM // 2, 1),
    )
    turned = (total * cosine + swapped * sine).astype(jnp.bfloat16)
    own_seg = seg_f[team][:, KPART : KPART + 1]
    keyval[2, :, :KVCOLS] = turned[:, QCOLS:]
    keyval[2, :, KVCOLS:] = jnp.broadcast_to(own_seg, (GROUP, 128)).astype(jnp.bfloat16)

    def key_copy(ahead):
        return pltpu.make_async_remote_copy(
            src_ref=keyval.at[2],
            dst_ref=keyval.at[2 - ahead],
            send_sem=key_send.at[ahead - 1],
            recv_sem=key_recv.at[ahead - 1],
            device_id=((dp + ahead) % NDP, inner),
            device_id_type=MESH,
        )

    for ahead in (1, 2):
        key_copy(ahead).start()
    for ahead in (1, 2):
        key_copy(ahead).wait_recv()

    count = 3 * GROUP
    window = keyval[...].reshape(count, KVCOLS + 128)
    key_block = window[:, :HEAD_DIM]
    value_block = window[:, HEAD_DIM:KVCOLS]
    nt = (((1,), (1,)), ((), ()))
    key_seg = lax.dot_general(
        jnp.ones((GROUP, 128), jnp.bfloat16),
        window[:, KVCOLS:],
        nt,
        preferred_element_type=jnp.float32,
    )
    row = lax.broadcasted_iota(jnp.int32, (GROUP, count), 0)
    key = lax.broadcasted_iota(jnp.int32, (GROUP, count), 1)
    distance = row + 2 * GROUP - key
    allowed = (
        (distance >= 0)
        & (distance < WINDOW)
        & (key + (dp - 2) * GROUP >= 0)
        & (key_seg == own_seg * 128.0)
    )
    for head in range(HEADS_HERE):
        scores = lax.dot_general(
            turned[:, head * HEAD_DIM : (head + 1) * HEAD_DIM],
            key_block,
            nt,
            preferred_element_type=jnp.float32,
        ) * HEAD_DIM ** (-0.5)
        scores = jnp.where(allowed, scores, -1e30)
        sink = sink_ref[head]
        row_max = jnp.maximum(jnp.max(scores, axis=-1, keepdims=True), sink)
        weights = jnp.exp(scores - row_max)
        denominator = jnp.sum(weights, axis=-1, keepdims=True) + jnp.exp(sink - row_max)
        probabilities = (weights / denominator).astype(jnp.bfloat16)
        mixed = jnp.dot(probabilities, value_block, preferred_element_type=jnp.float32)
        attended[team, :, head * HEAD_DIM : (head + 1) * HEAD_DIM] = mixed.astype(jnp.bfloat16)

    def att_copy(ahead):
        return pltpu.make_async_remote_copy(
            src_ref=attended.at[team],
            dst_ref=attended.at[team],
            send_sem=att_send.at[ahead - 1],
            recv_sem=att_recv.at[ahead - 1],
            device_id=(member(ahead)[1], inner),
            device_id_type=MESH,
        )

    for ahead in range(1, TEAM):
        att_copy(ahead).start()
    for ahead in range(1, TEAM):
        att_copy(ahead).wait_recv()
    projected = lax.dot_general(
        attended[...].reshape(TEAM * GROUP, QCOLS),
        wo_all[...].reshape(QUART, QCOLS),
        nt,
        preferred_element_type=jnp.float32,
    )
    out_part[...] = projected.reshape(TEAM * NI, ROWS, QUART).astype(jnp.bfloat16)

    def out_copy(index):
        other, other_dp = member(index // NI)
        other_in = (inner + index % NI) % NI
        return pltpu.make_async_remote_copy(
            src_ref=out_part.at[other * NI + other_in],
            dst_ref=out_in.at[team * NI + inner],
            send_sem=out_send.at[index],
            recv_sem=out_recv.at[index],
            device_id=(other_dp, other_in),
            device_id_type=MESH,
        )

    def start_out(index, carry):
        out_copy(index).start()
        return carry

    def wait_out(index, carry):
        out_copy(index).wait_recv()
        return carry

    lax.fori_loop(1, TEAM * NI, start_out, 0)
    out_in[team * NI + inner] = out_part[team * NI + inner]
    lax.fori_loop(1, TEAM * NI, wait_out, 0)
    summed = jnp.sum(
        out_in[...].astype(jnp.float32).reshape(TEAM, NI, ROWS, QUART), axis=1
    )
    for part in range(TEAM):
        wide[:, part * QUART : (part + 1) * QUART] = summed[part]
    for block in range(NX * NZ):
        wide_at, block_at = places(block)
        norm[:, block_at : block_at + KPART] = wide[:, wide_at : wide_at + KPART]
    res[...] = (tok_ref[...].astype(jnp.float32) + norm[...]).astype(jnp.bfloat16)

    bf16, f32 = jnp.bfloat16, jnp.float32
    nn = (((1,), (0,)), ((), ()))

    def iota(shape, dimension):
        return lax.broadcasted_iota(jnp.int32, shape, dimension)

    def ones_where(condition):
        return jnp.where(condition, 1.0, 0.0)

    half = z % 2
    chip_y = inner // 2
    core = inner % 2
    partner = x * NZ + z + 1 - 2 * half
    sibling = inner + 1 - 2 * core
    for load in loads:
        load.wait()

    values = res[...].astype(f32)
    mean_square = jnp.mean(values * values, axis=-1, keepdims=True)
    moe_in = (values * lax.rsqrt(mean_square + EPSILON) * moe_gain_ref[...].reshape(1, D)).astype(bf16)
    norm[...] = moe_in.astype(f32)
    halves[...] = jnp.zeros_like(halves)
    for part in range(2):
        halves[part, :, :HALF] = norm[:, part * HALF : (part + 1) * HALF]

    logits = lax.dot_general(moe_in, router[...], nt, preferred_element_type=f32)
    expert = iota((ROWS, EXPERTS), 1)
    route_row = iota((ROWS, EXPERTS), 0)
    named = []
    for k in range(4):
        match = jnp.zeros((ROWS, EXPERTS), f32)
        for number in range(ROWS):
            match = jnp.where(
                (route_row == number) & (expert == routes_ref[k, number]), 1.0, match
            )
        named.append(match)
    chosen = [jnp.sum(match * logits, axis=-1, keepdims=True) for match in named]
    largest = jnp.maximum(jnp.maximum(chosen[0], chosen[1]), jnp.maximum(chosen[2], chosen[3]))
    raised = [jnp.exp(value - largest) for value in chosen]
    whole = raised[0] + raised[1] + raised[2] + raised[3]
    onehot = named[0] + named[1] + named[2] + named[3]
    mix = (
        named[0] * raised[0] + named[1] * raised[1] + named[2] * raised[2] + named[3] * raised[3]
    ) / whole
    earlier = jnp.dot(
        ones_where(iota((ROWS, ROWS), 0) > iota((ROWS, ROWS), 1)),
        onehot,
        preferred_element_type=f32,
    )
    mix_high = mix.astype(bf16).astype(f32)
    mix_low = mix - mix_high
    column = iota((EXPERTS, 8 * 128), 1)
    source = iota((EXPERTS, 8 * 128), 0)
    table = jnp.zeros((ROWS, 8 * 128), f32)
    for slot in range(2):
        here = onehot * ones_where(earlier == slot)
        for kind, value in enumerate((here, here * mix_high, here * mix_low)):
            place = (source % 8) * 128 + TABLE + kind * 8 + (source // 8) * 2 + slot
            table = table + jnp.dot(
                value.astype(bf16),
                ones_where(column == place).astype(bf16),
                preferred_element_type=f32,
            )
    for other in range(NZ):
        part = other % 2
        pair = other // 2
        pay[other, :, :TAIL] = halves[part, :, :TAIL].astype(bf16)
        pay[other, :, TAIL:] = (
            halves[part, :, TAIL:] + table[:, pair * 128 : (pair + 1) * 128]
        ).astype(bf16)

    def z_copy(index):
        other = (z + index) % NZ
        return pltpu.make_async_remote_copy(
            src_ref=pay.at[other],
            dst_ref=gathered.at[z],
            send_sem=z_send.at[index],
            recv_sem=z_recv.at[index],
            device_id=(x * NZ + other, inner),
            device_id_type=MESH,
        )

    def start_z(index, carry):
        z_copy(index).start()
        return carry

    def wait_z(index, carry):
        z_copy(index).wait_recv()
        return carry

    lax.fori_loop(1, NZ, start_z, 0)
    gathered[z] = pay[z]

    bias_term = jnp.dot(mix, down_bias[...], precision=lax.Precision.HIGHEST)
    target = iota((2 * UNITS, 2 * UPAD), 1)
    place = iota((2 * UNITS, 2 * UPAD), 0)
    unweave = ones_where(target == place // 2 + (place % 2) * UPAD).astype(bf16)

    def sort_columns(index, carry):
        lines = pl.ds(pl.multiple_of(index * 144, 16), 144)
        gate_w[lines, :] = jnp.dot(gate_raw[lines, :], unweave, preferred_element_type=f32).astype(
            bf16
        )
        return carry

    lax.fori_loop(0, HALF // 144, sort_columns, 0)
    bias_row = gate_bias[pl.ds(dp // 2, 1), :]
    bias_high = bias_row.astype(bf16).astype(f32)
    bias_mid = (bias_row - bias_high).astype(bf16).astype(f32)
    bias_low = bias_row - bias_high - bias_mid
    line = iota((ROWS, 2 * UNITS), 0)
    bias_parts = jnp.where(
        line == 0, bias_high, jnp.where(line == 1, bias_mid, jnp.where(line == 2, bias_low, 0.0))
    )
    bias = jnp.sum(
        jnp.dot(bias_parts.astype(bf16), unweave, preferred_element_type=f32),
        axis=0,
        keepdims=True,
    )

    lax.fori_loop(1, NZ, wait_z, 0)
    row_total = NZ * ROWS
    near = gathered[...].astype(f32).reshape(row_total, HPAD)
    near_tail = near[:, TAIL:].astype(bf16)
    slot_row = iota((SLOTS, 128), 0)
    slot_lane = iota((SLOTS, 128), 1)
    select = lax.dot_general(
        ones_where(slot_lane - TABLE == slot_row // NZ).astype(bf16),
        near_tail,
        nt,
        preferred_element_type=f32,
    ) * ones_where(slot_row % NZ == slot_lane // ROWS)
    chosen_rows = jnp.dot(
        select.astype(bf16), near[:, :HALF].astype(bf16), preferred_element_type=f32
    )
    picked[...] = chosen_rows.astype(bf16).reshape(NX, 2 * NZ, HALF)

    def mix_matrix(kind):
        spread = jnp.dot(
            near_tail,
            ones_where(slot_row - TABLE - kind * 8 == slot_lane // NZ).astype(bf16),
            preferred_element_type=f32,
        )
        return (spread * ones_where(slot_row // ROWS == slot_lane % NZ)).astype(bf16)

    def x_copy(ahead):
        other = (x + ahead) % NX
        return pltpu.make_async_remote_copy(
            src_ref=picked.at[other],
            dst_ref=rows_all.at[inner, x],
            send_sem=x_send.at[ahead],
            recv_sem=x_recv.at[ahead],
            device_id=(other * NZ + z, inner),
            device_id_type=MESH,
        )

    def y_copy(ahead, back):
        block = rows_all.at[inner, (x + NX - back) % NX]
        return pltpu.make_async_remote_copy(
            src_ref=block,
            dst_ref=block,
            send_sem=y_send.at[ahead, back],
            recv_sem=y_recv.at[ahead, back],
            device_id=(dp, ((chip_y + ahead) % NY) * 2 + core),
            device_id_type=MESH,
        )

    def pass_copy(ahead, back):
        chip = (chip_y + NY - ahead) % NY
        block = rows_all.at[chip * 2 + core, (x + NX - back) % NX]
        return pltpu.make_async_remote_copy(
            src_ref=block,
            dst_ref=block,
            send_sem=y_send.at[2, back],
            recv_sem=y_recv.at[2, back],
            device_id=(dp, ((chip_y + ahead) % NY) * 2 + core),
            device_id_type=MESH,
        )

    def sib_copy(turn, chip):
        chunk = rows_all.at[chip * 2 + core]
        return pltpu.make_async_remote_copy(
            src_ref=chunk,
            dst_ref=chunk,
            send_sem=sib_send.at[turn],
            recv_sem=sib_recv.at[turn],
            device_id=(dp, sibling),
            device_id_type=MESH,
        )

    for ahead in range(1, NX):
        x_copy(ahead).start()
    rows_all[inner, x] = picked[x]
    for back in range(NX):
        if back:
            x_copy(back).wait_recv()
        for ahead in (1, 3):
            y_copy(ahead, back).start()
    sib_copy(0, chip_y).start()

    def gate_copy(chunk):
        return pltpu.make_async_remote_copy(
            src_ref=gate_own.at[chunk, 1 - half],
            dst_ref=gate_in.at[chunk],
            send_sem=gate_send.at[chunk],
            recv_sem=gate_recv.at[chunk],
            device_id=(partner, inner),
            device_id_type=MESH,
        )

    def hid_copy(chunk):
        return pltpu.make_async_remote_copy(
            src_ref=hidden.at[chunk, half],
            dst_ref=hidden.at[chunk, half],
            send_sem=hid_send.at[chunk],
            recv_sem=hid_recv.at[chunk],
            device_id=(partner, inner),
            device_id_type=MESH,
        )

    def fold_copy(turn):
        return pltpu.make_async_remote_copy(
            src_ref=sib_out.at[turn],
            dst_ref=sib_in.at[turn],
            send_sem=fold_send.at[turn],
            recv_sem=fold_recv.at[turn],
            device_id=(dp, sibling),
            device_id_type=MESH,
        )

    def pair_copy(turn, back):
        return pltpu.make_async_remote_copy(
            src_ref=pair_out.at[turn],
            dst_ref=pair_in.at[turn],
            send_sem=pair_send.at[turn],
            recv_sem=pair_recv.at[turn],
            device_id=(dp, ((chip_y + NY - back) % NY) * 2 + core),
            device_id_type=MESH,
        )

    def project(chunk):
        rows = rows_all[chunk].reshape(SLOTS, HALF)
        gate_own[chunk] = (
            jnp.dot(rows, gate_w[...], preferred_element_type=f32)
            .astype(bf16)
            .reshape(2, SLOTS // 2, 2 * UPAD)
        )
        gate_copy(chunk).start()

    def activate(chunk):
        gate_copy(chunk).wait_recv()
        gate_up = gate_own[chunk, half].astype(f32) + gate_in[chunk].astype(f32) + bias
        gate = jnp.minimum(gate_up[:, :UPAD], CLAMP_LIMIT)
        up = jnp.clip(gate_up[:, UPAD:], -CLAMP_LIMIT, CLAMP_LIMIT)
        hidden[chunk, half] = ((up + 1.0) * gate * jax.nn.sigmoid(GLU_SLOPE * gate)).astype(bf16)
        hid_copy(chunk).start()

    def lower(chunk):
        pl_wait = pltpu.make_async_remote_copy(
            src_ref=hidden.at[chunk, 1 - half],
            dst_ref=hidden.at[chunk, 1 - half],
            send_sem=hid_send.at[chunk],
            recv_sem=hid_recv.at[chunk],
            device_id=(partner, inner),
            device_id_type=MESH,
        )
        pl_wait.wait_recv()
        units = hidden[chunk].reshape(SLOTS, UPAD)[:, :UNITS]
        return jnp.dot(units, down_w[...], preferred_element_type=f32).astype(bf16)

    def turn_of(turn):
        back = (turn * (turn + 1) // 2) % NY
        return back, (chip_y + NY - back) % NY

    def step(turn, carry):
        @pl.when(turn < NY)
        def _():
            back, chip = turn_of(turn)

            @pl.when(turn > 0)
            def _():
                for block in range(NX):
                    y_copy(back, block).wait_recv()

                    @pl.when(back == (1 if block < 2 else 3))
                    def _():
                        pass_copy(back, block).start()

                sib_copy(turn, chip).start()

            project(chip * 2 + core)
            sib_copy(turn, chip).wait_recv()
            project(chip * 2 + 1 - core)

        @pl.when((turn >= 1) & (turn < NY + 1))
        def _():
            back, chip = turn_of(turn - 1)
            activate(chip * 2 + core)
            activate(chip * 2 + 1 - core)

        @pl.when(turn >= 2)
        def _():
            now = turn - 2
            back, chip = turn_of(now)
            sib_out[now] = lower(chip * 2 + 1 - core)
            fold_copy(now).start()
            kept = lower(chip * 2 + core).astype(f32)
            fold_copy(now).wait_recv()
            kept = kept + sib_in[now].astype(f32)

            @pl.when(now == 0)
            def _():
                sum_own[...] = kept

            @pl.when(now > 0)
            def _():
                pair_out[now] = kept.astype(bf16)
                pair_copy(now, back).start()

        return carry

    lax.fori_loop(0, NY + 2, step, 0)

    total = sum_own[...]
    for turn in range(1, NY):
        pair_copy(turn, (turn * (turn + 1) // 2) % NY).wait_recv()
        total = total + pair_in[turn].astype(f32)
    back_out[...] = total.astype(bf16).reshape(NX, 2 * NZ, HALF)

    def back_copy(ahead):
        other = (x + ahead) % NX
        return pltpu.make_async_remote_copy(
            src_ref=back_out.at[other],
            dst_ref=back_in.at[x],
            send_sem=back_send.at[ahead],
            recv_sem=back_recv.at[ahead],
            device_id=(other * NZ + z, inner),
            device_id_type=MESH,
        )

    for ahead in range(1, NX):
        back_copy(ahead).start()
    back_in[x] = back_out[x]
    for ahead in range(1, NX):
        back_copy(ahead).wait_recv()
    answers = back_in[...].reshape(SLOTS, HALF)
    combined = jnp.dot(mix_matrix(1), answers, preferred_element_type=f32) + jnp.dot(
        mix_matrix(2), answers, preferred_element_type=f32
    )
    mixed_out[...] = combined.reshape(NZ, ROWS, HALF).astype(bf16)

    def mix_copy(index):
        other = (z + index) % NZ
        return pltpu.make_async_remote_copy(
            src_ref=mixed_out.at[other],
            dst_ref=mixed_in.at[z],
            send_sem=mix_send.at[index],
            recv_sem=mix_recv.at[index],
            device_id=(x * NZ + other, inner),
            device_id_type=MESH,
        )

    def start_mix(index, carry):
        mix_copy(index).start()
        return carry

    def wait_mix(index, carry):
        mix_copy(index).wait_recv()
        return carry

    lax.fori_loop(1, NZ, start_mix, 0)
    mixed_in[z] = mixed_out[z]
    lax.fori_loop(1, NZ, wait_mix, 0)
    both = jnp.sum(mixed_in[...].astype(f32).reshape(NZ // 2, 2, ROWS, HALF), axis=0)
    for part in range(2):
        norm[:, part * HALF : (part + 1) * HALF] = both[part]
    out_ref[...] = (res[...].astype(f32) + norm[...] + bias_term).astype(bf16)


    for buffer, lane, towards, to, last in lanes:
        for step in range(1, last + 1):
            ring(buffer, lane, step, towards, to).wait_send()

    def wait_sends(index, carry):
        row_copy(index).wait_send()
        out_copy(index).wait_send()
        return carry

    lax.fori_loop(1, TEAM * NI, wait_sends, 0)
    for ahead in range(1, TEAM):
        part_copy(ahead).wait_send()
        att_copy(ahead).wait_send()
    for ahead in (1, 2):
        key_copy(ahead).wait_send()

    def wait_z_sends(index, carry):
        z_copy(index).wait_send()
        mix_copy(index).wait_send()
        return carry

    lax.fori_loop(1, NZ, wait_z_sends, 0)
    for ahead in range(1, NX):
        x_copy(ahead).wait_send()
        back_copy(ahead).wait_send()
    for ahead in range(1, NY):
        for block in range(NX):
            if ahead != 2:
                y_copy(ahead, block).wait_send()
            else:
                pass_copy(1 if block < 2 else 3, block).wait_send()
        pair_copy(ahead, (ahead * (ahead + 1) // 2) % NY).wait_send()

    def wait_turn(turn, carry):
        back, chip = turn_of(turn)
        sib_copy(turn, chip).wait_send()
        fold_copy(turn).wait_send()
        return carry

    def wait_chunk(chunk, carry):
        gate_copy(chunk).wait_send()
        hid_copy(chunk).wait_send()
        return carry

    lax.fori_loop(0, NY, wait_turn, 0)
    lax.fori_loop(0, NI, wait_chunk, 0)


def rope_tables(dp_index):
    half = HEAD_DIM // 2
    frequency = ROPE_BASE ** (-2.0 * jnp.arange(half, dtype=jnp.float32) / HEAD_DIM)
    positions = dp_index * GROUP + jnp.arange(GROUP, dtype=jnp.int32)
    angles = positions.astype(jnp.float32)[:, None] * frequency[None, :]
    cosine = jnp.cos(angles)
    sine = jnp.sin(angles)
    ones = jnp.ones((GROUP, HEAD_DIM), jnp.float32)
    head_cos = jnp.concatenate([cosine, cosine], axis=1)
    head_sin = jnp.concatenate([-sine, sine], axis=1)
    return (
        jnp.concatenate([head_cos, head_cos, head_cos, ones], axis=1),
        jnp.concatenate([head_sin, head_sin, head_sin, 0.0 * ones], axis=1),
    )


def per_device(
    tokens,
    segments,
    attn_gain,
    w_query,
    w_keyval,
    sink_logits,
    w_out,
    moe_gain,
    w_router,
    routes,
    w_gate_up,
    b_gate_up,
    w_down,
    b_down,
):
    dp_index = lax.axis_index("dp")
    cos_table, sin_table = rope_tables(dp_index)
    vmem = pl.BlockSpec(memory_space=pltpu.VMEM)
    smem = pl.BlockSpec(memory_space=pltpu.SMEM)
    anywhere = pl.BlockSpec(memory_space=pl.ANY)
    width = QCOLS + KVCOLS
    bf16, f32 = jnp.bfloat16, jnp.float32
    dma = pltpu.SemaphoreType.DMA
    buffers = [
        ((ROWS, D), f32),
        ((ROWS, TEAM * QUART), f32),
        ((TEAM, ROWS, QUART), bf16),
        ((TEAM * NI, ROWS, QUART), bf16),
        ((RING, KPAD, width), bf16),
        ((RING, KPAD, QCOLS), bf16),
        ((TEAM, GROUP, width), f32),
        ((TEAM, GROUP, width), bf16),
        ((TEAM - 1, GROUP, width), bf16),
        ((TEAM, GROUP, 128), f32),
        ((3, GROUP, KVCOLS + 128), bf16),
        ((TEAM, GROUP, QCOLS), bf16),
        ((TEAM * NI, ROWS, QUART), bf16),
        ((TEAM * NI, ROWS, QUART), bf16),
    ]
    semaphores = [(4, 4), (TEAM * NI,), (TEAM - 1,), (2,), (TEAM - 1,), (TEAM * NI,)]
    expert_inputs = [
        ((ROWS, D), bf16),
        ((EXPERTS, D), bf16),
        ((HALF, 2 * UNITS), bf16),
        ((HALF, 2 * UPAD), bf16),
        ((EXPERTS, 2 * UNITS), f32),
        ((UNITS, HALF), bf16),
        ((EXPERTS, D), f32),
    ]
    expert_buffers = [
        ((2, ROWS, HPAD), f32),
        ((NZ, ROWS, HPAD), bf16),
        ((NZ, ROWS, HPAD), bf16),
        ((NX, 2 * NZ, HALF), bf16),
        ((NI, NX, 2 * NZ, HALF), bf16),
        ((NI, 2, SLOTS // 2, 2 * UPAD), bf16),
        ((NI, SLOTS // 2, 2 * UPAD), bf16),
        ((NI, 2, SLOTS // 2, UPAD), bf16),
        ((NY, SLOTS, HALF), bf16),
        ((NY, SLOTS, HALF), bf16),
        ((NY, SLOTS, HALF), bf16),
        ((NY, SLOTS, HALF), bf16),
        ((SLOTS, HALF), f32),
        ((NX, 2 * NZ, HALF), bf16),
        ((NX, 2 * NZ, HALF), bf16),
        ((NZ, ROWS, HALF), bf16),
        ((NZ, ROWS, HALF), bf16),
    ]
    expert_semaphores = [(NZ,), (NX,), (NY, NX), (NY,), (NI,), (NI,), (NY,), (NY,), (NX,), (NZ,)]

    def allocate(shapes):
        return [pltpu.VMEM(shape, dtype) for shape, dtype in shapes]

    def pairs(shapes):
        return [dma(shape) for shape in shapes for _ in range(2)]

    return pl.pallas_call(
        layer_kernel,
        out_shape=jax.ShapeDtypeStruct((ROWS, D), bf16),
        in_specs=[vmem] * 2 + [smem] + [vmem] * 5 + [smem, vmem, smem] + [anywhere] * 5,
        out_specs=vmem,
        scratch_shapes=allocate(buffers)
        + pairs(semaphores)
        + allocate(expert_inputs)
        + [dma((5,))]
        + allocate(expert_buffers)
        + pairs(expert_semaphores),
        compiler_params=pltpu.CompilerParams(
            collective_id=0, has_side_effects=True, vmem_limit_bytes=56 * 2**20
        ),
        name="layer",
    )(
        tokens,
        attn_gain,
        segments,
        w_query,
        w_keyval,
        w_out.T,
        cos_table,
        sin_table,
        sink_logits,
        moe_gain,
        routes.T,
        w_router.T,
        w_gate_up,
        b_gate_up,
        w_down,
        b_down,
    )


def solution(mesh):
    return jax.shard_map(
        per_device,
        mesh=mesh,
        in_specs=(
            P(("dp", "inner"), None),
            P(("dp", "inner")),
            P(),
            P("dp", "inner"),
            P("dp", "inner"),
            P("inner"),
            P("inner", "dp"),
            P(),
            P(),
            P(("dp", "inner"), None),
            P("dp", "inner"),
            P(None, "inner"),
            P("inner", "dp"),
            P(),
        ),
        out_specs=P(("dp", "inner"), None),
        check_vma=False,
    )
```

```python
import functools
import jax
import jax.numpy as jnp
from jax import lax
from jax.experimental import pallas as pl
from jax.experimental.pallas import tpu as pltpu
from jax.sharding import PartitionSpec as P

HEAD_DIM = 64
WINDOW = 128
MESH = pl.DeviceIdType.MESH

EPSILON = 1e-05
ROPE_BASE = 150000.0
CLAMP_LIMIT = 7.0
GLU_SLOPE = 1.702

NX = 4
NZ = 16
NI = 8
NDP = NX * NZ
ROWS = 8
GROUP = ROWS * NI
KPART = 45
KPAD = 48
TEAM = 2 * NX
RING = NZ // 2
QUART = RING * KPAD
HEADS_HERE = 8
QCOLS = HEADS_HERE * HEAD_DIM
KVCOLS = 2 * HEAD_DIM
D = NX * NZ * KPART
HALF = D // 2
HPAD = 1536
TAIL = 1408
TABLE = HALF - TAIL
EXPERTS = 32
SLOTS = 2 * NX * NZ
UNITS = 360
UPAD = 384
NY = 4


def places(block):
    part = 2 * (block // NZ) + block % 2
    return part * QUART + (block % NZ) // 2 * KPAD, block * KPART


def layer_kernel(
    tok_ref,
    gain_ref,
    seg_ref,
    wq_ref,
    wkv_ref,
    wout_ref,
    cos_ref,
    sin_ref,
    sink_ref,
    moe_gain_ref,
    routes_ref,
    router_hbm,
    gate_hbm,
    gate_bias_hbm,
    down_hbm,
    down_bias_hbm,
    out_ref,
    norm,
    wide,
    quarter,
    rows_in,
    wq_all,
    wo_all,
    part_f,
    part_out,
    part_in,
    seg_f,
    keyval,
    attended,
    out_part,
    out_in,
    ring_send,
    ring_recv,
    row_send,
    row_recv,
    part_send,
    part_recv,
    key_send,
    key_recv,
    att_send,
    att_recv,
    out_send,
    out_recv,
    res,
    router,
    gate_raw,
    gate_w,
    gate_bias,
    down_w,
    down_bias,
    load_sem,
    halves,
    pay,
    gathered,
    picked,
    rows_all,
    gate_own,
    gate_in,
    hidden,
    sib_out,
    sib_in,
    pair_out,
    pair_in,
    sum_own,
    back_out,
    back_in,
    mixed_out,
    mixed_in,
    z_send,
    z_recv,
    x_send,
    x_recv,
    y_send,
    y_recv,
    sib_send,
    sib_recv,
    gate_send,
    gate_recv,
    hid_send,
    hid_recv,
    fold_send,
    fold_recv,
    pair_send,
    pair_recv,
    back_send,
    back_recv,
    mix_send,
    mix_recv,
):
    dp = lax.axis_index("dp")
    inner = lax.axis_index("inner")
    x = dp // NZ
    z = dp % NZ
    right = x * NZ + (z + 2) % NZ
    left = x * NZ + (z + NZ - 2) % NZ
    spot = z // 2
    team = 2 * x + z % 2

    def member(ahead):
        other = (team + ahead) % TEAM
        return other, (other // 2) * NZ + 2 * spot + other % 2

    barrier = pltpu.get_barrier_semaphore()

    def greet(index, carry):
        other, other_dp = member(index // NI)
        other_in = (inner + index % NI) % NI
        pl.semaphore_signal(barrier, inc=1, device_id=(other_dp, other_in), device_id_type=MESH)
        return carry

    lax.fori_loop(1, TEAM * NI, greet, 0)

    def greet_z(index, carry):
        other = x * NZ + (z + index) % NZ
        pl.semaphore_signal(barrier, inc=1, device_id=(other, inner), device_id_type=MESH)
        return carry

    lax.fori_loop(1, NZ, greet_z, 0)
    for other in (
        (dp + 1) % NDP,
        (dp + NDP - 1) % NDP,
        (dp + 2) % NDP,
        (dp + NDP - 2) % NDP,
    ):
        pl.semaphore_signal(barrier, inc=1, device_id=(other, inner), device_id_type=MESH)

    loads = [
        pltpu.make_async_copy(source, target, load_sem.at[number])
        for number, (source, target) in enumerate(
            (
                (router_hbm, router),
                (gate_hbm, gate_raw),
                (gate_bias_hbm, gate_bias),
                (down_hbm, down_w),
                (down_bias_hbm, down_bias),
            )
        )
    ]
    for load in loads:
        load.start()
    widen = jnp.where(
        lax.broadcasted_iota(jnp.int32, (KPAD, KPART), 0)
        == lax.broadcasted_iota(jnp.int32, (KPAD, KPART), 1),
        1.0,
        0.0,
    ).astype(jnp.bfloat16)
    for source, target, low, high in (
        (wq_ref, wq_all, 0, QCOLS),
        (wkv_ref, wq_all, QCOLS, QCOLS + KVCOLS),
        (wout_ref, wo_all, 0, QCOLS),
    ):
        target[spot, :, low:high] = jnp.dot(
            widen, source[...], preferred_element_type=jnp.float32
        ).astype(jnp.bfloat16)
    pl.semaphore_wait(barrier, TEAM * NI - 1 + NZ - 1 + 4)

    def ring(buffer, lane, step, towards, to):
        owner = (spot + RING - towards * (step - 1)) % RING
        return pltpu.make_async_remote_copy(
            src_ref=buffer.at[owner],
            dst_ref=buffer.at[owner],
            send_sem=ring_send.at[lane, step - 1],
            recv_sem=ring_recv.at[lane, step - 1],
            device_id=(to, inner),
            device_id_type=MESH,
        )

    lanes = (
        (wq_all, 0, 1, right, 4),
        (wq_all, 1, -1, left, 3),
        (wo_all, 2, 1, right, 3),
        (wo_all, 3, -1, left, 4),
    )
    for buffer, lane, towards, to, last in lanes:
        ring(buffer, lane, 1, towards, to).start()

    values = tok_ref[...].astype(jnp.float32)
    mean_square = jnp.mean(values * values, axis=-1, keepdims=True)
    norm[...] = values * lax.rsqrt(mean_square + EPSILON) * gain_ref[...].reshape(1, D)
    wide[...] = jnp.zeros_like(wide)
    for block in range(NX * NZ):
        wide_at, block_at = places(block)
        wide[:, wide_at : wide_at + KPART] = norm[:, block_at : block_at + KPART]
    row_number = lax.broadcasted_iota(jnp.int32, (ROWS, 1), 0)
    own_segments = jnp.zeros((ROWS, 1), jnp.float32)
    for number in range(ROWS):
        own_segments = jnp.where(
            row_number == number, seg_ref[number].astype(jnp.float32), own_segments
        )
    for part in range(TEAM):
        wide[:, part * QUART + KPART : part * QUART + KPART + 1] = own_segments
    for part in range(TEAM):
        quarter[part] = wide[:, part * QUART : (part + 1) * QUART].astype(jnp.bfloat16)

    def row_copy(index):
        other, other_dp = member(index // NI)
        other_in = (inner + index % NI) % NI
        return pltpu.make_async_remote_copy(
            src_ref=quarter.at[other],
            dst_ref=rows_in.at[team * NI + inner],
            send_sem=row_send.at[index],
            recv_sem=row_recv.at[index],
            device_id=(other_dp, other_in),
            device_id_type=MESH,
        )

    def start_row(index, carry):
        row_copy(index).start()
        return carry

    lax.fori_loop(1, TEAM * NI, start_row, 0)
    rows_in[team * NI + inner] = quarter[team]

    for step in range(1, RING // 2 + 1):
        for buffer, lane, towards, to, last in lanes:
            if step <= last:
                ring(buffer, lane, step, towards, to).wait_recv()
            if step + 1 <= last:
                ring(buffer, lane, step + 1, towards, to).start()

    def wait_row(index, carry):
        row_copy(index).wait_recv()
        return carry

    lax.fori_loop(1, TEAM * NI, wait_row, 0)

    all_rows = rows_in[...].astype(jnp.float32).reshape(TEAM * GROUP, QUART)
    seg_f[...] = all_rows[:, :128].reshape(TEAM, GROUP, 128)
    product = jnp.dot(
        all_rows.astype(jnp.bfloat16),
        wq_all[...].reshape(QUART, QCOLS + KVCOLS),
        preferred_element_type=jnp.float32,
    ).reshape(TEAM, GROUP, QCOLS + KVCOLS)
    part_f[...] = product
    part_out[...] = product.astype(jnp.bfloat16)

    def part_copy(ahead):
        other, other_dp = member(ahead)
        return pltpu.make_async_remote_copy(
            src_ref=part_out.at[other],
            dst_ref=part_in.at[ahead - 1],
            send_sem=part_send.at[ahead - 1],
            recv_sem=part_recv.at[ahead - 1],
            device_id=(other_dp, inner),
            device_id_type=MESH,
        )

    for ahead in range(1, TEAM):
        part_copy(ahead).start()
    total = part_f[team]
    for ahead in range(1, TEAM):
        part_copy(ahead).wait_recv()
        total = total + part_in[ahead - 1].astype(jnp.float32)

    width = QCOLS + KVCOLS
    cosine = jnp.concatenate([cos_ref[:, :128]] * 4 + [cos_ref[:, 128:]], axis=1)
    sine = jnp.concatenate([sin_ref[:, :128]] * 4 + [sin_ref[:, 128:]], axis=1)
    column = lax.broadcasted_iota(jnp.int32, (GROUP, width), 1)
    swapped = jnp.where(
        column % HEAD_DIM < HEAD_DIM // 2,
        pltpu.roll(total, width - HEAD_DIM // 2, 1),
        pltpu.roll(total, HEAD_DIM // 2, 1),
    )
    turned = (total * cosine + swapped * sine).astype(jnp.bfloat16)
    own_seg = seg_f[team][:, KPART : KPART + 1]
    keyval[2, :, :KVCOLS] = turned[:, QCOLS:]
    keyval[2, :, KVCOLS:] = jnp.broadcast_to(own_seg, (GROUP, 128)).astype(jnp.bfloat16)

    def key_copy(ahead):
        return pltpu.make_async_remote_copy(
            src_ref=keyval.at[2],
            dst_ref=keyval.at[2 - ahead],
            send_sem=key_send.at[ahead - 1],
            recv_sem=key_recv.at[ahead - 1],
            device_id=((dp + ahead) % NDP, inner),
            device_id_type=MESH,
        )

    for ahead in (1, 2):
        key_copy(ahead).start()
    for ahead in (1, 2):
        key_copy(ahead).wait_recv()

    count = 3 * GROUP
    window = keyval[...].reshape(count, KVCOLS + 128)
    key_block = window[:, :HEAD_DIM]
    value_block = window[:, HEAD_DIM:KVCOLS]
    nt = (((1,), (1,)), ((), ()))
    key_seg = lax.dot_general(
        jnp.ones((GROUP, 128), jnp.bfloat16),
        window[:, KVCOLS:],
        nt,
        preferred_element_type=jnp.float32,
    )
    row = lax.broadcasted_iota(jnp.int32, (GROUP, count), 0)
    key = lax.broadcasted_iota(jnp.int32, (GROUP, count), 1)
    distance = row + 2 * GROUP - key
    allowed = (
        (distance >= 0)
        & (distance < WINDOW)
        & (key + (dp - 2) * GROUP >= 0)
        & (key_seg == own_seg * 128.0)
    )
    for head in range(HEADS_HERE):
        scores = lax.dot_general(
            turned[:, head * HEAD_DIM : (head + 1) * HEAD_DIM],
            key_block,
            nt,
            preferred_element_type=jnp.float32,
        ) * HEAD_DIM ** (-0.5)
        scores = jnp.where(allowed, scores, -1e30)
        sink = sink_ref[head]
        row_max = jnp.maximum(jnp.max(scores, axis=-1, keepdims=True), sink)
        weights = jnp.exp(scores - row_max)
        denominator = jnp.sum(weights, axis=-1, keepdims=True) + jnp.exp(sink - row_max)
        probabilities = (weights / denominator).astype(jnp.bfloat16)
        mixed = jnp.dot(probabilities, value_block, preferred_element_type=jnp.float32)
        attended[team, :, head * HEAD_DIM : (head + 1) * HEAD_DIM] = mixed.astype(jnp.bfloat16)

    def att_copy(ahead):
        return pltpu.make_async_remote_copy(
            src_ref=attended.at[team],
            dst_ref=attended.at[team],
            send_sem=att_send.at[ahead - 1],
            recv_sem=att_recv.at[ahead - 1],
            device_id=(member(ahead)[1], inner),
            device_id_type=MESH,
        )

    for ahead in range(1, TEAM):
        att_copy(ahead).start()
    for ahead in range(1, TEAM):
        att_copy(ahead).wait_recv()
    projected = lax.dot_general(
        attended[...].reshape(TEAM * GROUP, QCOLS),
        wo_all[...].reshape(QUART, QCOLS),
        nt,
        preferred_element_type=jnp.float32,
    )
    out_part[...] = projected.reshape(TEAM * NI, ROWS, QUART).astype(jnp.bfloat16)

    def out_copy(index):
        other, other_dp = member(index // NI)
        other_in = (inner + index % NI) % NI
        return pltpu.make_async_remote_copy(
            src_ref=out_part.at[other * NI + other_in],
            dst_ref=out_in.at[team * NI + inner],
            send_sem=out_send.at[index],
            recv_sem=out_recv.at[index],
            device_id=(other_dp, other_in),
            device_id_type=MESH,
        )

    def start_out(index, carry):
        out_copy(index).start()
        return carry

    def wait_out(index, carry):
        out_copy(index).wait_recv()
        return carry

    lax.fori_loop(1, TEAM * NI, start_out, 0)
    out_in[team * NI + inner] = out_part[team * NI + inner]
    lax.fori_loop(1, TEAM * NI, wait_out, 0)
    summed = jnp.sum(
        out_in[...].astype(jnp.float32).reshape(TEAM, NI, ROWS, QUART), axis=1
    )
    for part in range(TEAM):
        wide[:, part * QUART : (part + 1) * QUART] = summed[part]
    for block in range(NX * NZ):
        wide_at, block_at = places(block)
        norm[:, block_at : block_at + KPART] = wide[:, wide_at : wide_at + KPART]
    res[...] = (tok_ref[...].astype(jnp.float32) + norm[...]).astype(jnp.bfloat16)

    bf16, f32 = jnp.bfloat16, jnp.float32
    nn = (((1,), (0,)), ((), ()))

    def iota(shape, dimension):
        return lax.broadcasted_iota(jnp.int32, shape, dimension)

    def ones_where(condition):
        return jnp.where(condition, 1.0, 0.0)

    half = z % 2
    chip_y = inner // 2
    core = inner % 2
    partner = x * NZ + z + 1 - 2 * half
    sibling = inner + 1 - 2 * core
    for load in loads:
        load.wait()

    values = res[...].astype(f32)
    mean_square = jnp.mean(values * values, axis=-1, keepdims=True)
    moe_in = (values * lax.rsqrt(mean_square + EPSILON) * moe_gain_ref[...].reshape(1, D)).astype(bf16)
    norm[...] = moe_in.astype(f32)
    halves[...] = jnp.zeros_like(halves)
    for part in range(2):
        halves[part, :, :HALF] = norm[:, part * HALF : (part + 1) * HALF]

    logits = lax.dot_general(moe_in, router[...], nt, preferred_element_type=f32)
    expert = iota((ROWS, EXPERTS), 1)
    route_row = iota((ROWS, EXPERTS), 0)
    named = []
    for k in range(4):
        match = jnp.zeros((ROWS, EXPERTS), f32)
        for number in range(ROWS):
            match = jnp.where(
                (route_row == number) & (expert == routes_ref[k, number]), 1.0, match
            )
        named.append(match)
    chosen = [jnp.sum(match * logits, axis=-1, keepdims=True) for match in named]
    largest = jnp.maximum(jnp.maximum(chosen[0], chosen[1]), jnp.maximum(chosen[2], chosen[3]))
    raised = [jnp.exp(value - largest) for value in chosen]
    whole = raised[0] + raised[1] + raised[2] + raised[3]
    onehot = named[0] + named[1] + named[2] + named[3]
    mix = (
        named[0] * raised[0] + named[1] * raised[1] + named[2] * raised[2] + named[3] * raised[3]
    ) / whole
    earlier = jnp.dot(
        ones_where(iota((ROWS, ROWS), 0) > iota((ROWS, ROWS), 1)),
        onehot,
        preferred_element_type=f32,
    )
    mix_high = mix.astype(bf16).astype(f32)
    mix_low = mix - mix_high
    column = iota((EXPERTS, 8 * 128), 1)
    source = iota((EXPERTS, 8 * 128), 0)
    table = jnp.zeros((ROWS, 8 * 128), f32)
    for slot in range(2):
        here = onehot * ones_where(earlier == slot)
        for kind, value in enumerate((here, here * mix_high, here * mix_low)):
            place = (source % 8) * 128 + TABLE + kind * 8 + (source // 8) * 2 + slot
            table = table + jnp.dot(
                value.astype(bf16),
                ones_where(column == place).astype(bf16),
                preferred_element_type=f32,
            )
    for other in range(NZ):
        part = other % 2
        pair = other // 2
        pay[other, :, :TAIL] = halves[part, :, :TAIL].astype(bf16)
        pay[other, :, TAIL:] = (
            halves[part, :, TAIL:] + table[:, pair * 128 : (pair + 1) * 128]
        ).astype(bf16)

    def z_copy(index):
        other = (z + index) % NZ
        return pltpu.make_async_remote_copy(
            src_ref=pay.at[other],
            dst_ref=gathered.at[z],
            send_sem=z_send.at[index],
            recv_sem=z_recv.at[index],
            device_id=(x * NZ + other, inner),
            device_id_type=MESH,
        )

    def start_z(index, carry):
        z_copy(index).start()
        return carry

    def wait_z(index, carry):
        z_copy(index).wait_recv()
        return carry

    lax.fori_loop(1, NZ, start_z, 0)
    gathered[z] = pay[z]

    bias_term = jnp.dot(mix, down_bias[...], precision=lax.Precision.HIGHEST)
    target = iota((2 * UNITS, 2 * UPAD), 1)
    place = iota((2 * UNITS, 2 * UPAD), 0)
    unweave = ones_where(target == place // 2 + (place % 2) * UPAD).astype(bf16)

    def sort_columns(index, carry):
        lines = pl.ds(pl.multiple_of(index * 144, 16), 144)
        gate_w[lines, :] = jnp.dot(gate_raw[lines, :], unweave, preferred_element_type=f32).astype(
            bf16
        )
        return carry

    lax.fori_loop(0, HALF // 144, sort_columns, 0)
    bias_row = gate_bias[pl.ds(dp // 2, 1), :]
    bias_high = bias_row.astype(bf16).astype(f32)
    bias_mid = (bias_row - bias_high).astype(bf16).astype(f32)
    bias_low = bias_row - bias_high - bias_mid
    line = iota((ROWS, 2 * UNITS), 0)
    bias_parts = jnp.where(
        line == 0, bias_high, jnp.where(line == 1, bias_mid, jnp.where(line == 2, bias_low, 0.0))
    )
    bias = jnp.sum(
        jnp.dot(bias_parts.astype(bf16), unweave, preferred_element_type=f32),
        axis=0,
        keepdims=True,
    )

    lax.fori_loop(1, NZ, wait_z, 0)
    row_total = NZ * ROWS
    near = gathered[...].astype(f32).reshape(row_total, HPAD)
    near_tail = near[:, TAIL:].astype(bf16)
    slot_row = iota((SLOTS, 128), 0)
    slot_lane = iota((SLOTS, 128), 1)
    select = lax.dot_general(
        ones_where(slot_lane - TABLE == slot_row // NZ).astype(bf16),
        near_tail,
        nt,
        preferred_element_type=f32,
    ) * ones_where(slot_row % NZ == slot_lane // ROWS)
    chosen_rows = jnp.dot(
        select.astype(bf16), near[:, :HALF].astype(bf16), preferred_element_type=f32
    )
    picked[...] = chosen_rows.astype(bf16).reshape(NX, 2 * NZ, HALF)

    def mix_matrix(kind):
        spread = jnp.dot(
            near_tail,
            ones_where(slot_row - TABLE - kind * 8 == slot_lane // NZ).astype(bf16),
            preferred_element_type=f32,
        )
        return (spread * ones_where(slot_row // ROWS == slot_lane % NZ)).astype(bf16)

    def x_copy(ahead):
        other = (x + ahead) % NX
        return pltpu.make_async_remote_copy(
            src_ref=picked.at[other],
            dst_ref=rows_all.at[inner, x],
            send_sem=x_send.at[ahead],
            recv_sem=x_recv.at[ahead],
            device_id=(other * NZ + z, inner),
            device_id_type=MESH,
        )

    def y_copy(ahead, back):
        block = rows_all.at[inner, (x + NX - back) % NX]
        return pltpu.make_async_remote_copy(
            src_ref=block,
            dst_ref=block,
            send_sem=y_send.at[ahead, back],
            recv_sem=y_recv.at[ahead, back],
            device_id=(dp, ((chip_y + ahead) % NY) * 2 + core),
            device_id_type=MESH,
        )

    def pass_copy(ahead, back):
        chip = (chip_y + NY - ahead) % NY
        block = rows_all.at[chip * 2 + core, (x + NX - back) % NX]
        return pltpu.make_async_remote_copy(
            src_ref=block,
            dst_ref=block,
            send_sem=y_send.at[2, back],
            recv_sem=y_recv.at[2, back],
            device_id=(dp, ((chip_y + ahead) % NY) * 2 + core),
            device_id_type=MESH,
        )

    def sib_copy(turn, chip):
        chunk = rows_all.at[chip * 2 + core]
        return pltpu.make_async_remote_copy(
            src_ref=chunk,
            dst_ref=chunk,
            send_sem=sib_send.at[turn],
            recv_sem=sib_recv.at[turn],
            device_id=(dp, sibling),
            device_id_type=MESH,
        )

    for ahead in range(1, NX):
        x_copy(ahead).start()
    rows_all[inner, x] = picked[x]
    for back in range(NX):
        if back:
            x_copy(back).wait_recv()
        for ahead in (1, 3):
            y_copy(ahead, back).start()
    sib_copy(0, chip_y).start()

    def gate_copy(chunk):
        return pltpu.make_async_remote_copy(
            src_ref=gate_own.at[chunk, 1 - half],
            dst_ref=gate_in.at[chunk],
            send_sem=gate_send.at[chunk],
            recv_sem=gate_recv.at[chunk],
            device_id=(partner, inner),
            device_id_type=MESH,
        )

    def hid_copy(chunk):
        return pltpu.make_async_remote_copy(
            src_ref=hidden.at[chunk, half],
            dst_ref=hidden.at[chunk, half],
            send_sem=hid_send.at[chunk],
            recv_sem=hid_recv.at[chunk],
            device_id=(partner, inner),
            device_id_type=MESH,
        )

    def fold_copy(turn):
        return pltpu.make_async_remote_copy(
            src_ref=sib_out.at[turn],
            dst_ref=sib_in.at[turn],
            send_sem=fold_send.at[turn],
            recv_sem=fold_recv.at[turn],
            device_id=(dp, sibling),
            device_id_type=MESH,
        )

    def pair_copy(turn, back):
        return pltpu.make_async_remote_copy(
            src_ref=pair_out.at[turn],
            dst_ref=pair_in.at[turn],
            send_sem=pair_send.at[turn],
            recv_sem=pair_recv.at[turn],
            device_id=(dp, ((chip_y + NY - back) % NY) * 2 + core),
            device_id_type=MESH,
        )

    def project(chunk):
        rows = rows_all[chunk].reshape(SLOTS, HALF)
        gate_own[chunk] = (
            jnp.dot(rows, gate_w[...], preferred_element_type=f32)
            .astype(bf16)
            .reshape(2, SLOTS // 2, 2 * UPAD)
        )
        gate_copy(chunk).start()

    def activate(chunk):
        gate_copy(chunk).wait_recv()
        gate_up = gate_own[chunk, half].astype(f32) + gate_in[chunk].astype(f32) + bias
        gate = jnp.minimum(gate_up[:, :UPAD], CLAMP_LIMIT)
        up = jnp.clip(gate_up[:, UPAD:], -CLAMP_LIMIT, CLAMP_LIMIT)
        hidden[chunk, half] = ((up + 1.0) * gate * jax.nn.sigmoid(GLU_SLOPE * gate)).astype(bf16)
        hid_copy(chunk).start()

    def lower(chunk):
        pl_wait = pltpu.make_async_remote_copy(
            src_ref=hidden.at[chunk, 1 - half],
            dst_ref=hidden.at[chunk, 1 - half],
            send_sem=hid_send.at[chunk],
            recv_sem=hid_recv.at[chunk],
            device_id=(partner, inner),
            device_id_type=MESH,
        )
        pl_wait.wait_recv()
        units = hidden[chunk].reshape(SLOTS, UPAD)[:, :UNITS]
        return jnp.dot(units, down_w[...], preferred_element_type=f32).astype(bf16)

    def turn_of(turn):
        back = (turn * (turn + 1) // 2) % NY
        return back, (chip_y + NY - back) % NY

    def step(turn, carry):
        @pl.when(turn < NY)
        def _():
            back, chip = turn_of(turn)

            @pl.when(turn > 0)
            def _():
                for block in range(NX):
                    y_copy(back, block).wait_recv()

                    @pl.when(back == (1 if block < 2 else 3))
                    def _():
                        pass_copy(back, block).start()

                sib_copy(turn, chip).start()

            project(chip * 2 + core)

        @pl.when((turn >= 1) & (turn < NY + 1))
        def _():
            back, chip = turn_of(turn - 1)
            sib_copy(turn - 1, chip).wait_recv()
            project(chip * 2 + 1 - core)

        @pl.when((turn >= 2) & (turn < NY + 2))
        def _():
            back, chip = turn_of(turn - 2)
            activate(chip * 2 + core)
            activate(chip * 2 + 1 - core)

        @pl.when((turn >= 3) & (turn < NY + 3))
        def _():
            now = turn - 3
            back, chip = turn_of(now)
            sib_out[now] = lower(chip * 2 + 1 - core)
            fold_copy(now).start()
            pair_out[now] = lower(chip * 2 + core)

        @pl.when(turn >= 4)
        def _():
            now = turn - 4
            back, chip = turn_of(now)
            fold_copy(now).wait_recv()
            kept = pair_out[now].astype(f32) + sib_in[now].astype(f32)

            @pl.when(now == 0)
            def _():
                sum_own[...] = kept

            @pl.when(now > 0)
            def _():
                pair_out[now] = kept.astype(bf16)
                pair_copy(now, back).start()

        return carry

    mix_high_rows = mix_matrix(1)
    mix_low_rows = mix_matrix(2)
    lax.fori_loop(0, NY + 4, step, 0)

    total = sum_own[...]
    for turn in range(1, NY):
        pair_copy(turn, (turn * (turn + 1) // 2) % NY).wait_recv()
        total = total + pair_in[turn].astype(f32)
    back_out[...] = total.astype(bf16).reshape(NX, 2 * NZ, HALF)

    def back_copy(ahead):
        other = (x + ahead) % NX
        return pltpu.make_async_remote_copy(
            src_ref=back_out.at[other],
            dst_ref=back_in.at[x],
            send_sem=back_send.at[ahead],
            recv_sem=back_recv.at[ahead],
            device_id=(other * NZ + z, inner),
            device_id_type=MESH,
        )

    for ahead in range(1, NX):
        back_copy(ahead).start()
    back_in[x] = back_out[x]
    for ahead in range(1, NX):
        back_copy(ahead).wait_recv()
    answers = back_in[...].reshape(SLOTS, HALF)
    combined = jnp.dot(mix_high_rows, answers, preferred_element_type=f32) + jnp.dot(
        mix_low_rows, answers, preferred_element_type=f32
    )
    mixed_out[...] = combined.reshape(NZ, ROWS, HALF).astype(bf16)

    def mix_copy(index):
        other = (z + index) % NZ
        return pltpu.make_async_remote_copy(
            src_ref=mixed_out.at[other],
            dst_ref=mixed_in.at[z],
            send_sem=mix_send.at[index],
            recv_sem=mix_recv.at[index],
            device_id=(x * NZ + other, inner),
            device_id_type=MESH,
        )

    def start_mix(index, carry):
        mix_copy(index).start()
        return carry

    def wait_mix(index, carry):
        mix_copy(index).wait_recv()
        return carry

    lax.fori_loop(1, NZ, start_mix, 0)
    mixed_in[z] = mixed_out[z]
    lax.fori_loop(1, NZ, wait_mix, 0)
    both = jnp.sum(mixed_in[...].astype(f32).reshape(NZ // 2, 2, ROWS, HALF), axis=0)
    for part in range(2):
        norm[:, part * HALF : (part + 1) * HALF] = both[part]
    out_ref[...] = (res[...].astype(f32) + norm[...] + bias_term).astype(bf16)


    for buffer, lane, towards, to, last in lanes:
        for step in range(1, last + 1):
            ring(buffer, lane, step, towards, to).wait_send()

    def wait_sends(index, carry):
        row_copy(index).wait_send()
        out_copy(index).wait_send()
        return carry

    lax.fori_loop(1, TEAM * NI, wait_sends, 0)
    for ahead in range(1, TEAM):
        part_copy(ahead).wait_send()
        att_copy(ahead).wait_send()
    for ahead in (1, 2):
        key_copy(ahead).wait_send()

    def wait_z_sends(index, carry):
        z_copy(index).wait_send()
        mix_copy(index).wait_send()
        return carry

    lax.fori_loop(1, NZ, wait_z_sends, 0)
    for ahead in range(1, NX):
        x_copy(ahead).wait_send()
        back_copy(ahead).wait_send()
    for ahead in range(1, NY):
        for block in range(NX):
            if ahead != 2:
                y_copy(ahead, block).wait_send()
            else:
                pass_copy(1 if block < 2 else 3, block).wait_send()
        pair_copy(ahead, (ahead * (ahead + 1) // 2) % NY).wait_send()

    def wait_turn(turn, carry):
        back, chip = turn_of(turn)
        sib_copy(turn, chip).wait_send()
        fold_copy(turn).wait_send()
        return carry

    def wait_chunk(chunk, carry):
        gate_copy(chunk).wait_send()
        hid_copy(chunk).wait_send()
        return carry

    lax.fori_loop(0, NY, wait_turn, 0)
    lax.fori_loop(0, NI, wait_chunk, 0)


def rope_tables(dp_index):
    half = HEAD_DIM // 2
    frequency = ROPE_BASE ** (-2.0 * jnp.arange(half, dtype=jnp.float32) / HEAD_DIM)
    positions = dp_index * GROUP + jnp.arange(GROUP, dtype=jnp.int32)
    angles = positions.astype(jnp.float32)[:, None] * frequency[None, :]
    cosine = jnp.cos(angles)
    sine = jnp.sin(angles)
    ones = jnp.ones((GROUP, HEAD_DIM), jnp.float32)
    head_cos = jnp.concatenate([cosine, cosine], axis=1)
    head_sin = jnp.concatenate([-sine, sine], axis=1)
    return (
        jnp.concatenate([head_cos, head_cos, head_cos, ones], axis=1),
        jnp.concatenate([head_sin, head_sin, head_sin, 0.0 * ones], axis=1),
    )


def per_device(
    tokens,
    segments,
    attn_gain,
    w_query,
    w_keyval,
    sink_logits,
    w_out,
    moe_gain,
    w_router,
    routes,
    w_gate_up,
    b_gate_up,
    w_down,
    b_down,
):
    dp_index = lax.axis_index("dp")
    cos_table, sin_table = rope_tables(dp_index)
    vmem = pl.BlockSpec(memory_space=pltpu.VMEM)
    smem = pl.BlockSpec(memory_space=pltpu.SMEM)
    anywhere = pl.BlockSpec(memory_space=pl.ANY)
    width = QCOLS + KVCOLS
    bf16, f32 = jnp.bfloat16, jnp.float32
    dma = pltpu.SemaphoreType.DMA
    buffers = [
        ((ROWS, D), f32),
        ((ROWS, TEAM * QUART), f32),
        ((TEAM, ROWS, QUART), bf16),
        ((TEAM * NI, ROWS, QUART), bf16),
        ((RING, KPAD, width), bf16),
        ((RING, KPAD, QCOLS), bf16),
        ((TEAM, GROUP, width), f32),
        ((TEAM, GROUP, width), bf16),
        ((TEAM - 1, GROUP, width), bf16),
        ((TEAM, GROUP, 128), f32),
        ((3, GROUP, KVCOLS + 128), bf16),
        ((TEAM, GROUP, QCOLS), bf16),
        ((TEAM * NI, ROWS, QUART), bf16),
        ((TEAM * NI, ROWS, QUART), bf16),
    ]
    semaphores = [(4, 4), (TEAM * NI,), (TEAM - 1,), (2,), (TEAM - 1,), (TEAM * NI,)]
    expert_inputs = [
        ((ROWS, D), bf16),
        ((EXPERTS, D), bf16),
        ((HALF, 2 * UNITS), bf16),
        ((HALF, 2 * UPAD), bf16),
        ((EXPERTS, 2 * UNITS), f32),
        ((UNITS, HALF), bf16),
        ((EXPERTS, D), f32),
    ]
    expert_buffers = [
        ((2, ROWS, HPAD), f32),
        ((NZ, ROWS, HPAD), bf16),
        ((NZ, ROWS, HPAD), bf16),
        ((NX, 2 * NZ, HALF), bf16),
        ((NI, NX, 2 * NZ, HALF), bf16),
        ((NI, 2, SLOTS // 2, 2 * UPAD), bf16),
        ((NI, SLOTS // 2, 2 * UPAD), bf16),
        ((NI, 2, SLOTS // 2, UPAD), bf16),
        ((NY, SLOTS, HALF), bf16),
        ((NY, SLOTS, HALF), bf16),
        ((NY, SLOTS, HALF), bf16),
        ((NY, SLOTS, HALF), bf16),
        ((SLOTS, HALF), f32),
        ((NX, 2 * NZ, HALF), bf16),
        ((NX, 2 * NZ, HALF), bf16),
        ((NZ, ROWS, HALF), bf16),
        ((NZ, ROWS, HALF), bf16),
    ]
    expert_semaphores = [(NZ,), (NX,), (NY, NX), (NY,), (NI,), (NI,), (NY,), (NY,), (NX,), (NZ,)]

    def allocate(shapes):
        return [pltpu.VMEM(shape, dtype) for shape, dtype in shapes]

    def pairs(shapes):
        return [dma(shape) for shape in shapes for _ in range(2)]

    return pl.pallas_call(
        layer_kernel,
        out_shape=jax.ShapeDtypeStruct((ROWS, D), bf16),
        in_specs=[vmem] * 2 + [smem] + [vmem] * 5 + [smem, vmem, smem] + [anywhere] * 5,
        out_specs=vmem,
        scratch_shapes=allocate(buffers)
        + pairs(semaphores)
        + allocate(expert_inputs)
        + [dma((5,))]
        + allocate(expert_buffers)
        + pairs(expert_semaphores),
        compiler_params=pltpu.CompilerParams(
            collective_id=0, has_side_effects=True, vmem_limit_bytes=56 * 2**20
        ),
        name="layer",
    )(
        tokens,
        attn_gain,
        segments,
        w_query,
        w_keyval,
        w_out.T,
        cos_table,
        sin_table,
        sink_logits,
        moe_gain,
        routes.T,
        w_router.T,
        w_gate_up,
        b_gate_up,
        w_down,
        b_down,
    )


def solution(mesh):
    return jax.shard_map(
        per_device,
        mesh=mesh,
        in_specs=(
            P(("dp", "inner"), None),
            P(("dp", "inner")),
            P(),
            P("dp", "inner"),
            P("dp", "inner"),
            P("inner"),
            P("inner", "dp"),
            P(),
            P(),
            P(("dp", "inner"), None),
            P("dp", "inner"),
            P(None, "inner"),
            P("inner", "dp"),
            P(),
        ),
        out_specs=P(("dp", "inner"), None),
        check_vma=False,
    )
```

```python
import functools
import jax
import jax.numpy as jnp
from jax import lax
from jax.experimental import pallas as pl
from jax.experimental.pallas import tpu as pltpu
from jax.sharding import PartitionSpec as P

HEAD_DIM = 64
WINDOW = 128
MESH = pl.DeviceIdType.MESH

EPSILON = 1e-05
ROPE_BASE = 150000.0
CLAMP_LIMIT = 7.0
GLU_SLOPE = 1.702

NX = 4
NZ = 16
NI = 8
NDP = NX * NZ
ROWS = 8
GROUP = ROWS * NI
KPART = 45
KPAD = 48
TEAM = 2 * NX
RING = NZ // 2
QUART = RING * KPAD
HEADS_HERE = 8
QCOLS = HEADS_HERE * HEAD_DIM
KVCOLS = 2 * HEAD_DIM
D = NX * NZ * KPART
HALF = D // 2
HPAD = 1536
TAIL = 1408
TABLE = HALF - TAIL
EXPERTS = 32
SLOTS = 2 * NX * NZ
UNITS = 360
UPAD = 384
NY = 4


def places(block):
    part = 2 * (block // NZ) + block % 2
    return part * QUART + (block % NZ) // 2 * KPAD, block * KPART


def layer_kernel(
    tok_ref,
    gain_ref,
    seg_ref,
    wq_ref,
    wkv_ref,
    wout_ref,
    cos_ref,
    sin_ref,
    sink_ref,
    moe_gain_ref,
    routes_ref,
    router_hbm,
    gate_hbm,
    gate_bias_hbm,
    down_hbm,
    down_bias_hbm,
    out_ref,
    norm,
    wide,
    quarter,
    rows_in,
    wq_all,
    wo_all,
    part_f,
    part_out,
    part_in,
    seg_f,
    keyval,
    attended,
    out_part,
    out_in,
    ring_send,
    ring_recv,
    row_send,
    row_recv,
    part_send,
    part_recv,
    key_send,
    key_recv,
    att_send,
    att_recv,
    out_send,
    out_recv,
    res,
    router,
    gate_raw,
    gate_w,
    gate_bias,
    down_w,
    down_bias,
    load_sem,
    halves,
    pay,
    gathered,
    picked,
    rows_all,
    gate_own,
    gate_in,
    hidden,
    sib_out,
    sib_in,
    pair_out,
    pair_in,
    sum_own,
    back_out,
    back_in,
    mixed_out,
    mixed_in,
    z_send,
    z_recv,
    x_send,
    x_recv,
    y_send,
    y_recv,
    sib_send,
    sib_recv,
    gate_send,
    gate_recv,
    hid_send,
    hid_recv,
    fold_send,
    fold_recv,
    pair_send,
    pair_recv,
    back_send,
    back_recv,
    mix_send,
    mix_recv,
):
    dp = lax.axis_index("dp")
    inner = lax.axis_index("inner")
    x = dp // NZ
    z = dp % NZ
    right = x * NZ + (z + 2) % NZ
    left = x * NZ + (z + NZ - 2) % NZ
    spot = z // 2
    team = 2 * x + z % 2

    def member(ahead):
        other = (team + ahead) % TEAM
        return other, (other // 2) * NZ + 2 * spot + other % 2

    barrier = pltpu.get_barrier_semaphore()

    def greet(index, carry):
        other, other_dp = member(index // NI)
        other_in = (inner + index % NI) % NI
        pl.semaphore_signal(barrier, inc=1, device_id=(other_dp, other_in), device_id_type=MESH)
        return carry

    lax.fori_loop(1, TEAM * NI, greet, 0)

    def greet_z(index, carry):
        other = x * NZ + (z + index) % NZ
        pl.semaphore_signal(barrier, inc=1, device_id=(other, inner), device_id_type=MESH)
        return carry

    lax.fori_loop(1, NZ, greet_z, 0)
    for other in (
        (dp + 1) % NDP,
        (dp + NDP - 1) % NDP,
        (dp + 2) % NDP,
        (dp + NDP - 2) % NDP,
    ):
        pl.semaphore_signal(barrier, inc=1, device_id=(other, inner), device_id_type=MESH)

    loads = [
        pltpu.make_async_copy(source, target, load_sem.at[number])
        for number, (source, target) in enumerate(
            (
                (router_hbm, router),
                (gate_hbm, gate_raw),
                (gate_bias_hbm, gate_bias),
                (down_hbm, down_w),
                (down_bias_hbm, down_bias),
            )
        )
    ]
    for load in loads:
        load.start()
    widen = jnp.where(
        lax.broadcasted_iota(jnp.int32, (KPAD, KPART), 0)
        == lax.broadcasted_iota(jnp.int32, (KPAD, KPART), 1),
        1.0,
        0.0,
    ).astype(jnp.bfloat16)
    for source, target, low, high in (
        (wq_ref, wq_all, 0, QCOLS),
        (wkv_ref, wq_all, QCOLS, QCOLS + KVCOLS),
        (wout_ref, wo_all, 0, QCOLS),
    ):
        target[spot, :, low:high] = jnp.dot(
            widen, source[...], preferred_element_type=jnp.float32
        ).astype(jnp.bfloat16)
    pl.semaphore_wait(barrier, TEAM * NI - 1 + NZ - 1 + 4)

    def ring(buffer, lane, step, towards, to):
        owner = (spot + RING - towards * (step - 1)) % RING
        return pltpu.make_async_remote_copy(
            src_ref=buffer.at[owner],
            dst_ref=buffer.at[owner],
            send_sem=ring_send.at[lane, step - 1],
            recv_sem=ring_recv.at[lane, step - 1],
            device_id=(to, inner),
            device_id_type=MESH,
        )

    lanes = (
        (wq_all, 0, 1, right, 4),
        (wq_all, 1, -1, left, 3),
        (wo_all, 2, 1, right, 3),
        (wo_all, 3, -1, left, 4),
    )
    for buffer, lane, towards, to, last in lanes:
        ring(buffer, lane, 1, towards, to).start()

    values = tok_ref[...].astype(jnp.float32)
    mean_square = jnp.mean(values * values, axis=-1, keepdims=True)
    norm[...] = values * lax.rsqrt(mean_square + EPSILON) * gain_ref[...].reshape(1, D)
    wide[...] = jnp.zeros_like(wide)
    for block in range(NX * NZ):
        wide_at, block_at = places(block)
        wide[:, wide_at : wide_at + KPART] = norm[:, block_at : block_at + KPART]
    row_number = lax.broadcasted_iota(jnp.int32, (ROWS, 1), 0)
    own_segments = jnp.zeros((ROWS, 1), jnp.float32)
    for number in range(ROWS):
        own_segments = jnp.where(
            row_number == number, seg_ref[number].astype(jnp.float32), own_segments
        )
    for part in range(TEAM):
        wide[:, part * QUART + KPART : part * QUART + KPART + 1] = own_segments
    for part in range(TEAM):
        quarter[part] = wide[:, part * QUART : (part + 1) * QUART].astype(jnp.bfloat16)

    def row_copy(index):
        other, other_dp = member(index // NI)
        other_in = (inner + index % NI) % NI
        return pltpu.make_async_remote_copy(
            src_ref=quarter.at[other],
            dst_ref=rows_in.at[team * NI + inner],
            send_sem=row_send.at[index],
            recv_sem=row_recv.at[index],
            device_id=(other_dp, other_in),
            device_id_type=MESH,
        )

    def start_row(index, carry):
        row_copy(index).start()
        return carry

    lax.fori_loop(1, TEAM * NI, start_row, 0)
    rows_in[team * NI + inner] = quarter[team]

    for step in range(1, RING // 2 + 1):
        for buffer, lane, towards, to, last in lanes:
            if step <= last:
                ring(buffer, lane, step, towards, to).wait_recv()
            if step + 1 <= last:
                ring(buffer, lane, step + 1, towards, to).start()

    def wait_row(index, carry):
        row_copy(index).wait_recv()
        return carry

    lax.fori_loop(1, TEAM * NI, wait_row, 0)

    all_rows = rows_in[...].astype(jnp.float32).reshape(TEAM * GROUP, QUART)
    seg_f[...] = all_rows[:, :128].reshape(TEAM, GROUP, 128)
    product = jnp.dot(
        all_rows.astype(jnp.bfloat16),
        wq_all[...].reshape(QUART, QCOLS + KVCOLS),
        preferred_element_type=jnp.float32,
    ).reshape(TEAM, GROUP, QCOLS + KVCOLS)
    part_f[...] = product
    part_out[...] = product.astype(jnp.bfloat16)

    def part_copy(ahead):
        other, other_dp = member(ahead)
        return pltpu.make_async_remote_copy(
            src_ref=part_out.at[other],
            dst_ref=part_in.at[ahead - 1],
            send_sem=part_send.at[ahead - 1],
            recv_sem=part_recv.at[ahead - 1],
            device_id=(other_dp, inner),
            device_id_type=MESH,
        )

    for ahead in range(1, TEAM):
        part_copy(ahead).start()
    total = part_f[team]
    for ahead in range(1, TEAM):
        part_copy(ahead).wait_recv()
        total = total + part_in[ahead - 1].astype(jnp.float32)

    width = QCOLS + KVCOLS
    cosine = jnp.concatenate([cos_ref[:, :128]] * 4 + [cos_ref[:, 128:]], axis=1)
    sine = jnp.concatenate([sin_ref[:, :128]] * 4 + [sin_ref[:, 128:]], axis=1)
    column = lax.broadcasted_iota(jnp.int32, (GROUP, width), 1)
    swapped = jnp.where(
        column % HEAD_DIM < HEAD_DIM // 2,
        pltpu.roll(total, width - HEAD_DIM // 2, 1),
        pltpu.roll(total, HEAD_DIM // 2, 1),
    )
    turned = (total * cosine + swapped * sine).astype(jnp.bfloat16)
    own_seg = seg_f[team][:, KPART : KPART + 1]
    keyval[2, :, :KVCOLS] = turned[:, QCOLS:]
    keyval[2, :, KVCOLS:] = jnp.broadcast_to(own_seg, (GROUP, 128)).astype(jnp.bfloat16)

    def key_copy(ahead):
        return pltpu.make_async_remote_copy(
            src_ref=keyval.at[2],
            dst_ref=keyval.at[2 - ahead],
            send_sem=key_send.at[ahead - 1],
            recv_sem=key_recv.at[ahead - 1],
            device_id=((dp + ahead) % NDP, inner),
            device_id_type=MESH,
        )

    for ahead in (1, 2):
        key_copy(ahead).start()
    for ahead in (1, 2):
        key_copy(ahead).wait_recv()

    count = 3 * GROUP
    window = keyval[...].reshape(count, KVCOLS + 128)
    key_block = window[:, :HEAD_DIM]
    value_block = window[:, HEAD_DIM:KVCOLS]
    nt = (((1,), (1,)), ((), ()))
    key_seg = lax.dot_general(
        jnp.ones((GROUP, 128), jnp.bfloat16),
        window[:, KVCOLS:],
        nt,
        preferred_element_type=jnp.float32,
    )
    row = lax.broadcasted_iota(jnp.int32, (GROUP, count), 0)
    key = lax.broadcasted_iota(jnp.int32, (GROUP, count), 1)
    distance = row + 2 * GROUP - key
    allowed = (
        (distance >= 0)
        & (distance < WINDOW)
        & (key + (dp - 2) * GROUP >= 0)
        & (key_seg == own_seg * 128.0)
    )
    for head in range(HEADS_HERE):
        scores = lax.dot_general(
            turned[:, head * HEAD_DIM : (head + 1) * HEAD_DIM],
            key_block,
            nt,
            preferred_element_type=jnp.float32,
        ) * HEAD_DIM ** (-0.5)
        scores = jnp.where(allowed, scores, -1e30)
        sink = sink_ref[head]
        row_max = jnp.maximum(jnp.max(scores, axis=-1, keepdims=True), sink)
        weights = jnp.exp(scores - row_max)
        denominator = jnp.sum(weights, axis=-1, keepdims=True) + jnp.exp(sink - row_max)
        probabilities = (weights / denominator).astype(jnp.bfloat16)
        mixed = jnp.dot(probabilities, value_block, preferred_element_type=jnp.float32)
        attended[team, :, head * HEAD_DIM : (head + 1) * HEAD_DIM] = mixed.astype(jnp.bfloat16)

    def att_copy(ahead):
        return pltpu.make_async_remote_copy(
            src_ref=attended.at[team],
            dst_ref=attended.at[team],
            send_sem=att_send.at[ahead - 1],
            recv_sem=att_recv.at[ahead - 1],
            device_id=(member(ahead)[1], inner),
            device_id_type=MESH,
        )

    for ahead in range(1, TEAM):
        att_copy(ahead).start()
    for ahead in range(1, TEAM):
        att_copy(ahead).wait_recv()
    projected = lax.dot_general(
        attended[...].reshape(TEAM * GROUP, QCOLS),
        wo_all[...].reshape(QUART, QCOLS),
        nt,
        preferred_element_type=jnp.float32,
    )
    out_part[...] = projected.reshape(TEAM * NI, ROWS, QUART).astype(jnp.bfloat16)

    def out_copy(index):
        other, other_dp = member(index // NI)
        other_in = (inner + index % NI) % NI
        return pltpu.make_async_remote_copy(
            src_ref=out_part.at[other * NI + other_in],
            dst_ref=out_in.at[team * NI + inner],
            send_sem=out_send.at[index],
            recv_sem=out_recv.at[index],
            device_id=(other_dp, other_in),
            device_id_type=MESH,
        )

    def start_out(index, carry):
        out_copy(index).start()
        return carry

    def wait_out(index, carry):
        out_copy(index).wait_recv()
        return carry

    lax.fori_loop(1, TEAM * NI, start_out, 0)
    out_in[team * NI + inner] = out_part[team * NI + inner]
    lax.fori_loop(1, TEAM * NI, wait_out, 0)
    summed = jnp.sum(
        out_in[...].astype(jnp.float32).reshape(TEAM, NI, ROWS, QUART), axis=1
    )
    for part in range(TEAM):
        wide[:, part * QUART : (part + 1) * QUART] = summed[part]
    for block in range(NX * NZ):
        wide_at, block_at = places(block)
        norm[:, block_at : block_at + KPART] = wide[:, wide_at : wide_at + KPART]
    res[...] = (tok_ref[...].astype(jnp.float32) + norm[...]).astype(jnp.bfloat16)

    bf16, f32 = jnp.bfloat16, jnp.float32
    nn = (((1,), (0,)), ((), ()))

    def iota(shape, dimension):
        return lax.broadcasted_iota(jnp.int32, shape, dimension)

    def ones_where(condition):
        return jnp.where(condition, 1.0, 0.0)

    half = z % 2
    chip_y = inner // 2
    core = inner % 2
    partner = x * NZ + z + 1 - 2 * half
    sibling = inner + 1 - 2 * core
    for load in loads:
        load.wait()

    values = res[...].astype(f32)
    mean_square = jnp.mean(values * values, axis=-1, keepdims=True)
    moe_in = (values * lax.rsqrt(mean_square + EPSILON) * moe_gain_ref[...].reshape(1, D)).astype(bf16)
    norm[...] = moe_in.astype(f32)
    halves[...] = jnp.zeros_like(halves)
    for part in range(2):
        halves[part, :, :HALF] = norm[:, part * HALF : (part + 1) * HALF]

    logits = lax.dot_general(moe_in, router[...], nt, preferred_element_type=f32)
    expert = iota((ROWS, EXPERTS), 1)
    route_row = iota((ROWS, EXPERTS), 0)
    named = []
    for k in range(4):
        match = jnp.zeros((ROWS, EXPERTS), f32)
        for number in range(ROWS):
            match = jnp.where(
                (route_row == number) & (expert == routes_ref[k, number]), 1.0, match
            )
        named.append(match)
    chosen = [jnp.sum(match * logits, axis=-1, keepdims=True) for match in named]
    largest = jnp.maximum(jnp.maximum(chosen[0], chosen[1]), jnp.maximum(chosen[2], chosen[3]))
    raised = [jnp.exp(value - largest) for value in chosen]
    whole = raised[0] + raised[1] + raised[2] + raised[3]
    onehot = named[0] + named[1] + named[2] + named[3]
    mix = (
        named[0] * raised[0] + named[1] * raised[1] + named[2] * raised[2] + named[3] * raised[3]
    ) / whole
    earlier = jnp.dot(
        ones_where(iota((ROWS, ROWS), 0) > iota((ROWS, ROWS), 1)),
        onehot,
        preferred_element_type=f32,
    )
    mix_high = mix.astype(bf16).astype(f32)
    mix_low = mix - mix_high
    column = iota((EXPERTS, 8 * 128), 1)
    source = iota((EXPERTS, 8 * 128), 0)
    table = jnp.zeros((ROWS, 8 * 128), f32)
    for slot in range(2):
        here = onehot * ones_where(earlier == slot)
        for kind, value in enumerate((here, here * mix_high, here * mix_low)):
            place = (source % 8) * 128 + TABLE + kind * 8 + (source // 8) * 2 + slot
            table = table + jnp.dot(
                value.astype(bf16),
                ones_where(column == place).astype(bf16),
                preferred_element_type=f32,
            )
    for other in range(NZ):
        part = other % 2
        pair = other // 2
        pay[other, :, :TAIL] = halves[part, :, :TAIL].astype(bf16)
        pay[other, :, TAIL:] = (
            halves[part, :, TAIL:] + table[:, pair * 128 : (pair + 1) * 128]
        ).astype(bf16)

    def z_copy(index):
        other = (z + index) % NZ
        return pltpu.make_async_remote_copy(
            src_ref=pay.at[other],
            dst_ref=gathered.at[z],
            send_sem=z_send.at[index],
            recv_sem=z_recv.at[index],
            device_id=(x * NZ + other, inner),
            device_id_type=MESH,
        )

    def far_first(index):
        return NZ // 2 + (index // 2) * (2 * (index % 2) - 1)

    def start_z(index, carry):
        z_copy(far_first(index)).start()
        return carry

    def wait_z(index, carry):
        z_copy(index).wait_recv()
        return carry

    lax.fori_loop(1, NZ, start_z, 0)
    gathered[z] = pay[z]

    bias_term = jnp.dot(mix, down_bias[...], precision=lax.Precision.HIGHEST)
    target = iota((2 * UNITS, 2 * UPAD), 1)
    place = iota((2 * UNITS, 2 * UPAD), 0)
    unweave = ones_where(target == place // 2 + (place % 2) * UPAD).astype(bf16)

    def sort_columns(index, carry):
        lines = pl.ds(pl.multiple_of(index * 144, 16), 144)
        gate_w[lines, :] = jnp.dot(gate_raw[lines, :], unweave, preferred_element_type=f32).astype(
            bf16
        )
        return carry

    lax.fori_loop(0, HALF // 144, sort_columns, 0)
    bias_row = gate_bias[pl.ds(dp // 2, 1), :]
    bias_high = bias_row.astype(bf16).astype(f32)
    bias_mid = (bias_row - bias_high).astype(bf16).astype(f32)
    bias_low = bias_row - bias_high - bias_mid
    line = iota((ROWS, 2 * UNITS), 0)
    bias_parts = jnp.where(
        line == 0, bias_high, jnp.where(line == 1, bias_mid, jnp.where(line == 2, bias_low, 0.0))
    )
    bias = jnp.sum(
        jnp.dot(bias_parts.astype(bf16), unweave, preferred_element_type=f32),
        axis=0,
        keepdims=True,
    )

    lax.fori_loop(1, NZ, wait_z, 0)
    row_total = NZ * ROWS
    near = gathered[...].astype(f32).reshape(row_total, HPAD)
    near_tail = near[:, TAIL:].astype(bf16)
    slot_row = iota((SLOTS, 128), 0)
    slot_lane = iota((SLOTS, 128), 1)
    select = lax.dot_general(
        ones_where(slot_lane - TABLE == slot_row // NZ).astype(bf16),
        near_tail,
        nt,
        preferred_element_type=f32,
    ) * ones_where(slot_row % NZ == slot_lane // ROWS)
    chosen_rows = jnp.dot(
        select.astype(bf16), near[:, :HALF].astype(bf16), preferred_element_type=f32
    )
    picked[...] = chosen_rows.astype(bf16).reshape(NX, 2 * NZ, HALF)

    def mix_matrix(kind):
        spread = jnp.dot(
            near_tail,
            ones_where(slot_row - TABLE - kind * 8 == slot_lane // NZ).astype(bf16),
            preferred_element_type=f32,
        )
        return (spread * ones_where(slot_row // ROWS == slot_lane % NZ)).astype(bf16)

    def x_copy(ahead):
        other = (x + ahead) % NX
        return pltpu.make_async_remote_copy(
            src_ref=picked.at[other],
            dst_ref=rows_all.at[inner, x],
            send_sem=x_send.at[ahead],
            recv_sem=x_recv.at[ahead],
            device_id=(other * NZ + z, inner),
            device_id_type=MESH,
        )

    def y_copy(ahead, back):
        block = rows_all.at[inner, (x + NX - back) % NX]
        return pltpu.make_async_remote_copy(
            src_ref=block,
            dst_ref=block,
            send_sem=y_send.at[ahead, back],
            recv_sem=y_recv.at[ahead, back],
            device_id=(dp, ((chip_y + ahead) % NY) * 2 + core),
            device_id_type=MESH,
        )

    def pass_copy(ahead, back):
        chip = (chip_y + NY - ahead) % NY
        block = rows_all.at[chip * 2 + core, (x + NX - back) % NX]
        return pltpu.make_async_remote_copy(
            src_ref=block,
            dst_ref=block,
            send_sem=y_send.at[2, back],
            recv_sem=y_recv.at[2, back],
            device_id=(dp, ((chip_y + ahead) % NY) * 2 + core),
            device_id_type=MESH,
        )

    def sib_copy(turn, chip):
        chunk = rows_all.at[chip * 2 + core]
        return pltpu.make_async_remote_copy(
            src_ref=chunk,
            dst_ref=chunk,
            send_sem=sib_send.at[turn],
            recv_sem=sib_recv.at[turn],
            device_id=(dp, sibling),
            device_id_type=MESH,
        )

    for ahead in range(1, NX):
        x_copy(ahead).start()
    rows_all[inner, x] = picked[x]
    for back in range(NX):
        if back:
            x_copy(back).wait_recv()
        for ahead in (1, 3):
            y_copy(ahead, back).start()
    sib_copy(0, chip_y).start()

    def gate_copy(chunk):
        return pltpu.make_async_remote_copy(
            src_ref=gate_own.at[chunk, 1 - half],
            dst_ref=gate_in.at[chunk],
            send_sem=gate_send.at[chunk],
            recv_sem=gate_recv.at[chunk],
            device_id=(partner, inner),
            device_id_type=MESH,
        )

    def hid_copy(chunk):
        return pltpu.make_async_remote_copy(
            src_ref=hidden.at[chunk, half],
            dst_ref=hidden.at[chunk, half],
            send_sem=hid_send.at[chunk],
            recv_sem=hid_recv.at[chunk],
            device_id=(partner, inner),
            device_id_type=MESH,
        )

    def fold_copy(turn):
        return pltpu.make_async_remote_copy(
            src_ref=sib_out.at[turn],
            dst_ref=sib_in.at[turn],
            send_sem=fold_send.at[turn],
            recv_sem=fold_recv.at[turn],
            device_id=(dp, sibling),
            device_id_type=MESH,
        )

    def pair_copy(turn, back):
        return pltpu.make_async_remote_copy(
            src_ref=pair_out.at[turn],
            dst_ref=pair_in.at[turn],
            send_sem=pair_send.at[turn],
            recv_sem=pair_recv.at[turn],
            device_id=(dp, ((chip_y + NY - back) % NY) * 2 + core),
            device_id_type=MESH,
        )

    def project(chunk):
        rows = rows_all[chunk].reshape(SLOTS, HALF)
        gate_own[chunk] = (
            jnp.dot(rows, gate_w[...], preferred_element_type=f32)
            .astype(bf16)
            .reshape(2, SLOTS // 2, 2 * UPAD)
        )
        gate_copy(chunk).start()

    def activate(chunk):
        gate_copy(chunk).wait_recv()
        gate_up = gate_own[chunk, half].astype(f32) + gate_in[chunk].astype(f32) + bias
        gate = jnp.minimum(gate_up[:, :UPAD], CLAMP_LIMIT)
        up = jnp.clip(gate_up[:, UPAD:], -CLAMP_LIMIT, CLAMP_LIMIT)
        hidden[chunk, half] = ((up + 1.0) * gate * jax.nn.sigmoid(GLU_SLOPE * gate)).astype(bf16)
        hid_copy(chunk).start()

    def lower(chunk):
        pl_wait = pltpu.make_async_remote_copy(
            src_ref=hidden.at[chunk, 1 - half],
            dst_ref=hidden.at[chunk, 1 - half],
            send_sem=hid_send.at[chunk],
            recv_sem=hid_recv.at[chunk],
            device_id=(partner, inner),
            device_id_type=MESH,
        )
        pl_wait.wait_recv()
        units = hidden[chunk].reshape(SLOTS, UPAD)[:, :UNITS]
        return jnp.dot(units, down_w[...], preferred_element_type=f32).astype(bf16)

    def turn_of(turn):
        back = (turn * (turn + 1) // 2) % NY
        return back, (chip_y + NY - back) % NY

    def step(turn, carry):
        @pl.when(turn < NY)
        def _():
            back, chip = turn_of(turn)

            @pl.when(turn > 0)
            def _():
                for block in range(NX):
                    y_copy(back, block).wait_recv()

                    @pl.when(back == (1 if block < 2 else 3))
                    def _():
                        pass_copy(back, block).start()

                sib_copy(turn, chip).start()

            project(chip * 2 + core)

        @pl.when((turn >= 1) & (turn < NY + 1))
        def _():
            back, chip = turn_of(turn - 1)
            sib_copy(turn - 1, chip).wait_recv()
            project(chip * 2 + 1 - core)

        @pl.when((turn >= 2) & (turn < NY + 2))
        def _():
            back, chip = turn_of(turn - 2)
            activate(chip * 2 + core)
            activate(chip * 2 + 1 - core)

        @pl.when((turn >= 3) & (turn < NY + 3))
        def _():
            now = turn - 3
            back, chip = turn_of(now)
            sib_out[now] = lower(chip * 2 + 1 - core)
            fold_copy(now).start()
            pair_out[now] = lower(chip * 2 + core)

        @pl.when(turn >= 4)
        def _():
            now = turn - 4
            back, chip = turn_of(now)
            fold_copy(now).wait_recv()
            kept = pair_out[now].astype(f32) + sib_in[now].astype(f32)

            @pl.when(now == 0)
            def _():
                sum_own[...] = kept

            @pl.when(now > 0)
            def _():
                pair_out[now] = kept.astype(bf16)
                pair_copy(now, back).start()

        return carry

    mix_high_rows = mix_matrix(1)
    mix_low_rows = mix_matrix(2)
    lax.fori_loop(0, NY + 4, step, 0)

    total = sum_own[...]
    for turn in range(1, NY):
        pair_copy(turn, (turn * (turn + 1) // 2) % NY).wait_recv()
        total = total + pair_in[turn].astype(f32)
    back_out[...] = total.astype(bf16).reshape(NX, 2 * NZ, HALF)

    def back_copy(ahead):
        other = (x + ahead) % NX
        return pltpu.make_async_remote_copy(
            src_ref=back_out.at[other],
            dst_ref=back_in.at[x],
            send_sem=back_send.at[ahead],
            recv_sem=back_recv.at[ahead],
            device_id=(other * NZ + z, inner),
            device_id_type=MESH,
        )

    for ahead in range(1, NX):
        back_copy(ahead).start()
    back_in[x] = back_out[x]
    for ahead in range(1, NX):
        back_copy(ahead).wait_recv()
    answers = back_in[...].reshape(SLOTS, HALF)
    combined = jnp.dot(mix_high_rows, answers, preferred_element_type=f32) + jnp.dot(
        mix_low_rows, answers, preferred_element_type=f32
    )
    mixed_out[...] = combined.reshape(NZ, ROWS, HALF).astype(bf16)

    def mix_copy(index):
        other = (z + index) % NZ
        return pltpu.make_async_remote_copy(
            src_ref=mixed_out.at[other],
            dst_ref=mixed_in.at[z],
            send_sem=mix_send.at[index],
            recv_sem=mix_recv.at[index],
            device_id=(x * NZ + other, inner),
            device_id_type=MESH,
        )

    def start_mix(index, carry):
        mix_copy(far_first(index)).start()
        return carry

    def wait_mix(index, carry):
        mix_copy(index).wait_recv()
        return carry

    lax.fori_loop(1, NZ, start_mix, 0)
    mixed_in[z] = mixed_out[z]
    lax.fori_loop(1, NZ, wait_mix, 0)
    both = jnp.sum(mixed_in[...].astype(f32).reshape(NZ // 2, 2, ROWS, HALF), axis=0)
    for part in range(2):
        norm[:, part * HALF : (part + 1) * HALF] = both[part]
    out_ref[...] = (res[...].astype(f32) + norm[...] + bias_term).astype(bf16)


    for buffer, lane, towards, to, last in lanes:
        for step in range(1, last + 1):
            ring(buffer, lane, step, towards, to).wait_send()

    def wait_sends(index, carry):
        row_copy(index).wait_send()
        out_copy(index).wait_send()
        return carry

    lax.fori_loop(1, TEAM * NI, wait_sends, 0)
    for ahead in range(1, TEAM):
        part_copy(ahead).wait_send()
        att_copy(ahead).wait_send()
    for ahead in (1, 2):
        key_copy(ahead).wait_send()

    def wait_z_sends(index, carry):
        z_copy(index).wait_send()
        mix_copy(index).wait_send()
        return carry

    lax.fori_loop(1, NZ, wait_z_sends, 0)
    for ahead in range(1, NX):
        x_copy(ahead).wait_send()
        back_copy(ahead).wait_send()
    for ahead in range(1, NY):
        for block in range(NX):
            if ahead != 2:
                y_copy(ahead, block).wait_send()
            else:
                pass_copy(1 if block < 2 else 3, block).wait_send()
        pair_copy(ahead, (ahead * (ahead + 1) // 2) % NY).wait_send()

    def wait_turn(turn, carry):
        back, chip = turn_of(turn)
        sib_copy(turn, chip).wait_send()
        fold_copy(turn).wait_send()
        return carry

    def wait_chunk(chunk, carry):
        gate_copy(chunk).wait_send()
        hid_copy(chunk).wait_send()
        return carry

    lax.fori_loop(0, NY, wait_turn, 0)
    lax.fori_loop(0, NI, wait_chunk, 0)


def rope_tables(dp_index):
    half = HEAD_DIM // 2
    frequency = ROPE_BASE ** (-2.0 * jnp.arange(half, dtype=jnp.float32) / HEAD_DIM)
    positions = dp_index * GROUP + jnp.arange(GROUP, dtype=jnp.int32)
    angles = positions.astype(jnp.float32)[:, None] * frequency[None, :]
    cosine = jnp.cos(angles)
    sine = jnp.sin(angles)
    ones = jnp.ones((GROUP, HEAD_DIM), jnp.float32)
    head_cos = jnp.concatenate([cosine, cosine], axis=1)
    head_sin = jnp.concatenate([-sine, sine], axis=1)
    return (
        jnp.concatenate([head_cos, head_cos, head_cos, ones], axis=1),
        jnp.concatenate([head_sin, head_sin, head_sin, 0.0 * ones], axis=1),
    )


def per_device(
    tokens,
    segments,
    attn_gain,
    w_query,
    w_keyval,
    sink_logits,
    w_out,
    moe_gain,
    w_router,
    routes,
    w_gate_up,
    b_gate_up,
    w_down,
    b_down,
):
    dp_index = lax.axis_index("dp")
    cos_table, sin_table = rope_tables(dp_index)
    vmem = pl.BlockSpec(memory_space=pltpu.VMEM)
    smem = pl.BlockSpec(memory_space=pltpu.SMEM)
    anywhere = pl.BlockSpec(memory_space=pl.ANY)
    width = QCOLS + KVCOLS
    bf16, f32 = jnp.bfloat16, jnp.float32
    dma = pltpu.SemaphoreType.DMA
    buffers = [
        ((ROWS, D), f32),
        ((ROWS, TEAM * QUART), f32),
        ((TEAM, ROWS, QUART), bf16),
        ((TEAM * NI, ROWS, QUART), bf16),
        ((RING, KPAD, width), bf16),
        ((RING, KPAD, QCOLS), bf16),
        ((TEAM, GROUP, width), f32),
        ((TEAM, GROUP, width), bf16),
        ((TEAM - 1, GROUP, width), bf16),
        ((TEAM, GROUP, 128), f32),
        ((3, GROUP, KVCOLS + 128), bf16),
        ((TEAM, GROUP, QCOLS), bf16),
        ((TEAM * NI, ROWS, QUART), bf16),
        ((TEAM * NI, ROWS, QUART), bf16),
    ]
    semaphores = [(4, 4), (TEAM * NI,), (TEAM - 1,), (2,), (TEAM - 1,), (TEAM * NI,)]
    expert_inputs = [
        ((ROWS, D), bf16),
        ((EXPERTS, D), bf16),
        ((HALF, 2 * UNITS), bf16),
        ((HALF, 2 * UPAD), bf16),
        ((EXPERTS, 2 * UNITS), f32),
        ((UNITS, HALF), bf16),
        ((EXPERTS, D), f32),
    ]
    expert_buffers = [
        ((2, ROWS, HPAD), f32),
        ((NZ, ROWS, HPAD), bf16),
        ((NZ, ROWS, HPAD), bf16),
        ((NX, 2 * NZ, HALF), bf16),
        ((NI, NX, 2 * NZ, HALF), bf16),
        ((NI, 2, SLOTS // 2, 2 * UPAD), bf16),
        ((NI, SLOTS // 2, 2 * UPAD), bf16),
        ((NI, 2, SLOTS // 2, UPAD), bf16),
        ((NY, SLOTS, HALF), bf16),
        ((NY, SLOTS, HALF), bf16),
        ((NY, SLOTS, HALF), bf16),
        ((NY, SLOTS, HALF), bf16),
        ((SLOTS, HALF), f32),
        ((NX, 2 * NZ, HALF), bf16),
        ((NX, 2 * NZ, HALF), bf16),
        ((NZ, ROWS, HALF), bf16),
        ((NZ, ROWS, HALF), bf16),
    ]
    expert_semaphores = [(NZ,), (NX,), (NY, NX), (NY,), (NI,), (NI,), (NY,), (NY,), (NX,), (NZ,)]

    def allocate(shapes):
        return [pltpu.VMEM(shape, dtype) for shape, dtype in shapes]

    def pairs(shapes):
        return [dma(shape) for shape in shapes for _ in range(2)]

    return pl.pallas_call(
        layer_kernel,
        out_shape=jax.ShapeDtypeStruct((ROWS, D), bf16),
        in_specs=[vmem] * 2 + [smem] + [vmem] * 5 + [smem, vmem, smem] + [anywhere] * 5,
        out_specs=vmem,
        scratch_shapes=allocate(buffers)
        + pairs(semaphores)
        + allocate(expert_inputs)
        + [dma((5,))]
        + allocate(expert_buffers)
        + pairs(expert_semaphores),
        compiler_params=pltpu.CompilerParams(
            collective_id=0, has_side_effects=True, vmem_limit_bytes=56 * 2**20
        ),
        name="layer",
    )(
        tokens,
        attn_gain,
        segments,
        w_query,
        w_keyval,
        w_out.T,
        cos_table,
        sin_table,
        sink_logits,
        moe_gain,
        routes.T,
        w_router.T,
        w_gate_up,
        b_gate_up,
        w_down,
        b_down,
    )


def solution(mesh):
    return jax.shard_map(
        per_device,
        mesh=mesh,
        in_specs=(
            P(("dp", "inner"), None),
            P(("dp", "inner")),
            P(),
            P("dp", "inner"),
            P("dp", "inner"),
            P("inner"),
            P("inner", "dp"),
            P(),
            P(),
            P(("dp", "inner"), None),
            P("dp", "inner"),
            P(None, "inner"),
            P("inner", "dp"),
            P(),
        ),
        out_specs=P(("dp", "inner"), None),
        check_vma=False,
    )
```
